32 devices in a mesh: grp: 8 (over z, core), sp: 4 (over y, x).
Axes of the slice: x: 2, y: 2, z: 4, core: 2. Of those that a mesh axis runs over, the one named last changes fastest.
Arguments:
- acts: bfloat16 [32, 4, 16, 728], P('grp', 'sp'), may hold values from -6 to 6
- cotangent: bfloat16 [32, 4, 16, 728], P(('grp', 'sp')), may hold values from -6 to 6
- depth_kernel: float32 [3, 3, 728], replicated, may hold values from -2 to 2
- point_weight: bfloat16 [728, 728], replicated, may hold values from -0.21875 to 0.21875
- batch_norm_gain: float32 [728], replicated, may hold values from 0.5 to 2
- norm_shift_bias: float32 [728], replicated, may hold values from -1 to 1
Outputs:
- block_out: bfloat16 [32, 4, 16, 728], P(('grp', 'sp'))
- input_grad: bfloat16 [32, 4, 16, 728], P('grp', 'sp')
- weight_grad: float32 [529984], P('sp')
The draws below stay inside these ranges and needn't reach their ends.
All inputs are finite; a program needn't handle non-finite values.
Results may differ from the reference program's by a relative error of at most 0.018.
Values may be sent and summed in bfloat16 or wider, within the bound.
A program may use at most 64 MiB of HBM per device.

```python
import math
import jax
import jax.numpy as jnp
from jax import lax

C = 728
COLS = 16
ROWS = 4
BATCH = 32
N_GRP = 8
N_SP = 4


def block_scale(stream_key, extent, pieces, least, largest):
    loudness, own = 1.0, jax.random.fold_in(stream_key, 6)
    for axis_at, blocks in pieces:
        draws = jnp.exp(jax.random.uniform(jax.random.fold_in(own, axis_at), (blocks,), jnp.float32, least / len(pieces), largest / len(pieces)))
        loudness = loudness * jnp.repeat(draws, extent[axis_at] // blocks).reshape([-1 if axis == axis_at else 1 for axis in range(len(extent))])
    return loudness


def centred(stream_key, shape, deviation, bound, cuts=(), dtype=jnp.bfloat16):
    array = deviation * jax.random.normal(stream_key, shape, jnp.float32)
    if cuts:
        array = array * block_scale(stream_key, shape, cuts, -0.22, 0.18)
    return jnp.clip(array, -bound, bound).astype(dtype)


def setup_inputs(seed: int = 0) -> dict:
    seeds = jax.random.split(jax.random.key(seed), 7)
    acts = centred(seeds[0], (BATCH, ROWS, COLS, C), 1.0, 6.0, ((0, 8), (1, 4)))
    cotangent = centred(seeds[1], (BATCH, ROWS, COLS, C), 1.0, 6.0, ((0, 32),))
    depth_kernel = centred(seeds[2], (3, 3, C), 9 ** -0.5, 2.0, (), jnp.float32)
    point_weight = centred(seeds[3], (C, C), C ** -0.5, 0.21875)
    batch_norm_gain = jnp.clip(jnp.exp(jax.random.uniform(seeds[4], (C,), jnp.float32, math.log(0.5), math.log(2.0))), 0.5, 2.0)
    norm_shift_bias = jnp.clip(jax.random.uniform(seeds[5], (C,), jnp.float32, -1.0, 1.0), -1.0, 1.0)
    return {"acts": acts, "cotangent": cotangent, "depth_kernel": depth_kernel, "point_weight": point_weight, "batch_norm_gain": batch_norm_gain, "norm_shift_bias": norm_shift_bias}


def depth_forward(field, filter_weight):
    rows = field.shape[1]
    cols = field.shape[2]
    padded = jnp.pad(field, ((0, 0), (1, 1), (1, 1), (0, 0)))
    total = jnp.zeros(field.shape, jnp.float32)
    for i in range(3):
        for j in range(3):
            total = total + padded[:, i:i + rows, j:j + cols, :] * filter_weight[i, j]
    return total

def depth_backward(field, filter_weight):
    rows = field.shape[1]
    cols = field.shape[2]
    padded = jnp.pad(field, ((0, 0), (1, 1), (1, 1), (0, 0)))
    total = jnp.zeros(field.shape, jnp.float32)
    for i in range(3):
        for j in range(3):
            total = total + padded[:, 2 - i:2 - i + rows, 2 - j:2 - j + cols, :] * filter_weight[i, j]
    return total

def one_group(carry, pair, depth_kernel, point_weight, batch_norm_gain, norm_shift_bias):
    inputs, grads = pair
    channel_count = inputs.shape[-1]
    sample_count = inputs.shape[0]
    input_single_precision = inputs.astype(jnp.float32)
    hidden = jnp.maximum(input_single_precision, 0.0)
    depthed = depth_forward(hidden, depth_kernel).astype(jnp.bfloat16)
    flat_d = depthed.reshape(-1, channel_count)
    element_count = flat_d.shape[0]
    projected_output = jnp.dot(flat_d, point_weight, preferred_element_type=jnp.float32)
    batch_mean = lax.optimization_barrier(jnp.sum(projected_output, axis=0)) / element_count
    var = lax.optimization_barrier(jnp.sum(projected_output * projected_output, axis=0)) / element_count - batch_mean * batch_mean
    inverse_deviation = lax.rsqrt(var + 1e-05)
    normalized_input = (projected_output - batch_mean) * inverse_deviation
    layer_outputs = (input_single_precision.reshape(-1, channel_count) + batch_norm_gain * normalized_input + norm_shift_bias).astype(jnp.bfloat16)
    gfloat = grads.astype(jnp.float32).reshape(-1, channel_count)
    scaled_output = gfloat * batch_norm_gain
    leading_layer = lax.optimization_barrier(jnp.sum(scaled_output, axis=0)) / element_count
    second_layer = lax.optimization_barrier(jnp.sum(scaled_output * normalized_input, axis=0)) / element_count
    projected_gradient = (inverse_deviation * (scaled_output - leading_layer - normalized_input * second_layer)).astype(jnp.bfloat16)
    per_device = flat_d.astype(jnp.float32).reshape(sample_count, -1, channel_count)
    per_group = projected_gradient.astype(jnp.float32).reshape(sample_count, -1, channel_count)
    term_list = jnp.einsum('ayu,ayq->auq', per_device, per_group).astype(jnp.bfloat16)
    term_list = lax.optimization_barrier(term_list).astype(jnp.float32)
    local_weight = lax.optimization_barrier(jnp.sum(term_list, axis=0))
    ddepth = jnp.dot(projected_gradient, point_weight.T, preferred_element_type=jnp.float32).reshape(inputs.shape)
    dhidden = depth_backward(ddepth, depth_kernel)
    dinput = (gfloat.reshape(inputs.shape) + jnp.where(inputs > 0, dhidden, 0.0)).astype(jnp.bfloat16)
    return (carry + local_weight, (layer_outputs.reshape(inputs.shape), dinput))

def reference(acts, cotangent, depth_kernel, point_weight, batch_norm_gain, norm_shift_bias):
    channel_count = acts.shape[-1]
    shape_g = (N_GRP, N_SP) + acts.shape[1:]
    xs = (acts.reshape(shape_g), cotangent.reshape(shape_g))

    def stepper(carry, pair):
        return one_group(carry, pair, depth_kernel, point_weight, batch_norm_gain, norm_shift_bias)
    wsum, pair_out = lax.scan(stepper, jnp.zeros((channel_count, channel_count), jnp.float32), xs)
    block_out = pair_out[0].reshape(acts.shape)
    input_grad = pair_out[1].reshape(acts.shape)
    return (block_out, input_grad, wsum.reshape(-1))
```

```python
import functools

import jax
import jax.numpy as jnp
from jax import lax
from jax.experimental import pallas as pl
from jax.experimental.pallas import tpu as pltpu
from jax.sharding import PartitionSpec as P

MESH = pl.DeviceIdType.MESH
LANES = 128
NT = (((1,), (1,)), ((), ()))


def lane_blocks(channels):
    return [slice(at, min(at + LANES, channels)) for at in range(0, channels, LANES)]


def column_shift(field, step):
    cols = field.shape[0]
    at = lax.broadcasted_iota(jnp.int32, field.shape, 0)
    keep = (at >= 1) if step > 0 else (at < cols - 1)
    return jnp.where(keep, pltpu.roll(field, step % cols, 0), 0.0)


def kernel(
    n_sp, n_grp, n_core, part_rows,
    acts_ref, cot_ref, dk_ref, pw_hbm, gain_ref, bias_ref,
    block_out_ref, input_grad_ref, weight_ref,
    ga, gc, pw, d_ref, p_ref, dp_ref, dsel_ref, dd_ref,
    pair_send, pair_recv, own_ref, z_send, z_recv, res_ref,
    local_sem, a_send, a_recv, c_send, c_recv,
    pair_ssem, pair_rsem, z_ssem, z_rsem, g_ssem, g_rsem, f_ssem, f_rsem,
):
    sp = lax.axis_index("sp")
    grp = lax.axis_index("grp")
    n_z = n_grp // n_core
    z, core = grp // n_core, grp % n_core
    other = (core + 1) % n_core
    partner = z * n_core + other
    n_rows, n_samples, cols, channels = ga.shape
    count = n_rows * n_samples * cols
    blocks = lane_blocks(channels)

    load_pw = pltpu.make_async_copy(pw_hbm, pw, local_sem.at[0])
    load_pw.start()
    own_acts = pltpu.make_async_copy(acts_ref.at[:, 0], ga.at[sp], local_sem.at[1])
    own_acts.start()
    own_cot = pltpu.make_async_copy(cot_ref.at[0], gc.at[sp], local_sem.at[2])
    own_cot.start()

    barrier = pltpu.get_barrier_semaphore()
    peers = [{"sp": (sp + k) % n_sp} for k in range(1, n_sp)]
    peers += [{"grp": ((z + k) % n_z) * n_core + core} for k in range(1, n_z)]
    peers += [{"grp": partner}]
    for peer in peers:
        pl.semaphore_signal(barrier, inc=1, device_id=peer, device_id_type=MESH)
    pl.semaphore_wait(barrier, len(peers))

    def acts_copy(k, slot, to):
        return pltpu.make_async_remote_copy(
            src_ref=acts_ref.at[:, 0], dst_ref=ga.at[slot],
            send_sem=a_send.at[k], recv_sem=a_recv.at[slot],
            device_id={"sp": to}, device_id_type=MESH,
        )

    def cot_copy(k, slot, to):
        return pltpu.make_async_remote_copy(
            src_ref=cot_ref.at[0], dst_ref=gc.at[slot],
            send_sem=c_send.at[k], recv_sem=c_recv.at[slot],
            device_id={"sp": to}, device_id_type=MESH,
        )

    for k in range(1, n_sp):
        acts_copy(k, sp, (sp + k) % n_sp).start()
    for k in range(1, n_sp):
        cot_copy(k, sp, (sp + k) % n_sp).start()

    dp_ref[0] = jnp.zeros(dp_ref.shape[1:], dp_ref.dtype)
    dp_ref[n_rows + 1] = jnp.zeros(dp_ref.shape[1:], dp_ref.dtype)
    own_acts.wait()
    load_pw.wait()
    for k in range(1, n_sp):
        acts_copy(k, (sp + k) % n_sp, sp).wait_recv()

    @pl.loop(0, n_samples)
    def _(b):
        for lanes in blocks:
            h = [jnp.maximum(ga[r, b, :, lanes].astype(jnp.float32), 0.0) for r in range(n_rows)]
            taps = [[dk_ref[i, j : j + 1, lanes] for j in range(3)] for i in range(3)]
            for r in range(n_rows):
                t = [
                    sum(h[r + i - 1] * taps[i][j] for i in range(3) if 0 <= r + i - 1 < n_rows)
                    for j in range(3)
                ]
                total = t[1] + column_shift(t[0], 1) + column_shift(t[2], -1)
                at = pl.multiple_of((r * n_samples + b) * cols, cols)
                d_ref[pl.ds(at, cols), lanes] = total.astype(jnp.bfloat16)

    p_ref[...] = jnp.dot(
        d_ref[...], pw[...], preferred_element_type=jnp.float32
    ).reshape(p_ref.shape)
    sel_rows = dsel_ref.shape[0]
    width = channels // n_sp
    row = lax.broadcasted_iota(jnp.int32, (sel_rows, channels), 0)
    lane = lax.broadcasted_iota(jnp.int32, (sel_rows, channels), 1)
    pick = jnp.where((lane - sp * width == row) & (row < width), 1.0, 0.0).astype(jnp.bfloat16)
    dsel_ref[...] = lax.dot_general(
        pick, d_ref[...], NT, preferred_element_type=jnp.float32
    ).astype(jnp.bfloat16)

    own_cot.wait()
    for k in range(1, n_sp):
        cot_copy(k, (sp + k) % n_sp, sp).wait_recv()

    means, rstds = [], []
    for lanes in blocks:
        size = lanes.stop - lanes.start
        s1 = s2 = sg = sgp = jnp.zeros((cols, size), jnp.float32)
        for r in range(n_rows):
            for b in range(n_samples):
                p = p_ref[r, b * cols : (b + 1) * cols, lanes]
                g = gc[b, r, :, lanes].astype(jnp.float32)
                s1, s2, sg, sgp = s1 + p, s2 + p * p, sg + g, sgp + g * p
        s1, s2, sg, sgp = [jnp.sum(s, axis=0, keepdims=True) for s in (s1, s2, sg, sgp)]
        gain = gain_ref[:, lanes]
        mean = s1 / count
        var = s2 / count - mean * mean
        rstd = lax.rsqrt(var + 1e-05)
        a1 = gain * sg / count
        a2 = gain * rstd * (sgp - mean * sg) / count
        means.append(mean)
        rstds.append(rstd)
        for r in range(n_rows):
            for b in range(n_samples):
                p = p_ref[r, b * cols : (b + 1) * cols, lanes]
                g = gc[b, r, :, lanes].astype(jnp.float32)
                xhat = (p - mean) * rstd
                dp_ref[r + 1, b * cols : (b + 1) * cols, lanes] = (
                    rstd * (g * gain - a1 - xhat * a2)
                ).astype(jnp.bfloat16)

    half = n_z * part_rows

    def product(which):
        left = dsel_ref[pl.ds(pl.multiple_of(which * half, half), half), :]
        return jnp.dot(
            left, dp_ref[1 : n_rows + 1].reshape(-1, channels), preferred_element_type=jnp.float32
        ).reshape(n_z, part_rows, channels)

    def pair_copy(k):
        return pltpu.make_async_remote_copy(
            src_ref=pair_send.at[k], dst_ref=pair_recv.at[k],
            send_sem=pair_ssem.at[k], recv_sem=pair_rsem.at[k],
            device_id={"grp": partner}, device_id_type=MESH,
        )

    def z_copy(k, slot, to):
        return pltpu.make_async_remote_copy(
            src_ref=z_send.at[k], dst_ref=z_recv.at[slot],
            send_sem=z_ssem.at[k], recv_sem=z_rsem.at[slot],
            device_id={"grp": to * n_core + core}, device_id_type=MESH,
        )

    def gather_copy(k, slot, to):
        return pltpu.make_async_remote_copy(
            src_ref=res_ref.at[core, slot], dst_ref=res_ref.at[core, slot],
            send_sem=g_ssem.at[k], recv_sem=g_rsem.at[slot],
            device_id={"grp": to * n_core + core}, device_id_type=MESH,
        )

    def forward_copy(slot, side):
        return pltpu.make_async_remote_copy(
            src_ref=res_ref.at[side, slot], dst_ref=res_ref.at[side, slot],
            send_sem=f_ssem.at[slot], recv_sem=f_rsem.at[slot],
            device_id={"grp": partner}, device_id_type=MESH,
        )

    pair_send[...] = product(other).astype(jnp.bfloat16)
    for k in range(n_z):
        pair_copy((z + 1 + k) % n_z).start()
    own_ref[...] = product(core)
    for k in range(1, n_z):
        to = (z + k) % n_z
        pair_copy(to).wait_recv()
        z_send[to] = (own_ref[to] + pair_recv[to].astype(jnp.float32)).astype(jnp.bfloat16)
        z_copy(to, z, to).start()

    dd_ref[...] = lax.dot_general(
        dp_ref[pl.ds(sp, 3)].reshape(-1, channels), pw[...], NT,
        preferred_element_type=jnp.float32,
    ).reshape(dd_ref.shape)

    pair_copy(z).wait_recv()
    mine = own_ref[z] + pair_recv[z].astype(jnp.float32)
    for k in range(1, n_z):
        slot = (z + k) % n_z
        z_copy(slot, slot, z).wait_recv()
        mine = mine + z_recv[slot].astype(jnp.float32)
    res_ref[core, z] = mine.astype(jnp.bfloat16)
    for k in range(1, n_z):
        gather_copy(k, z, (z + k) % n_z).start()
    forward_copy(z, core).start()

    for at, lanes in enumerate(blocks):
        taps = [[dk_ref[i, j : j + 1, lanes] for j in range(3)] for i in range(3)]
        gain, bias = gain_ref[:, lanes], bias_ref[:, lanes]
        for b in range(n_samples):
            own = slice(b * cols, (b + 1) * cols)
            dd = [dd_ref[i, own, lanes] for i in range(3)]
            t = [sum(dd[2 - i] * taps[i][j] for i in range(3)) for j in range(3)]
            dh = t[1] + column_shift(t[0], -1) + column_shift(t[2], 1)
            a = ga[sp, b, :, lanes].astype(jnp.float32)
            g = gc[b, sp, :, lanes].astype(jnp.float32)
            input_grad_ref[b, 0, :, lanes] = (g + jnp.where(a > 0, dh, 0.0)).astype(jnp.bfloat16)
        for r in range(n_rows):
            p = p_ref[r, pl.ds(pl.multiple_of(sp * cols, cols), cols), lanes]
            a = ga[r, sp, :, lanes].astype(jnp.float32)
            block_out_ref[0, r, :, lanes] = (
                a + gain * ((p - means[at]) * rstds[at]) + bias
            ).astype(jnp.bfloat16)

    for k in range(1, n_z):
        slot = (z + k) % n_z
        gather_copy(k, slot, z).wait_recv()
        forward_copy(slot, core).start()
    for k in range(n_z):
        forward_copy((z + k) % n_z, other).wait_recv()

    for side in range(n_core):
        for slot in range(n_z):
            at = (side * n_z + slot) * part_rows
            size = min(part_rows, width - at)
            weight_ref[at : at + size] = res_ref[side, slot, :size].astype(jnp.float32)

    for k in range(1, n_sp):
        acts_copy(k, sp, (sp + k) % n_sp).wait_send()
        cot_copy(k, sp, (sp + k) % n_sp).wait_send()
    for k in range(n_z):
        pair_copy(k).wait_send()
        forward_copy(k, core).wait_send()
    for k in range(1, n_z):
        z_copy((z + k) % n_z, z, (z + k) % n_z).wait_send()
        gather_copy(k, z, (z + k) % n_z).wait_send()


def fused(acts, cotangent, depth_kernel, point_weight, gain, bias):
    n_sp, n_grp, n_core = lax.axis_size("sp"), lax.axis_size("grp"), 2
    n_samples, _, cols, channels = acts.shape
    n_rows = cotangent.shape[1]
    n_z = n_grp // n_core
    width = channels // n_sp
    part_rows = -(-width // (n_grp * 8)) * 8
    bf16, f32 = jnp.bfloat16, jnp.float32
    vmem, dma = pltpu.VMEM, pltpu.SemaphoreType.DMA
    in_vmem, anywhere = pl.BlockSpec(memory_space=pltpu.VMEM), pl.BlockSpec(memory_space=pl.ANY)
    rows = n_samples * cols
    out = pl.pallas_call(
        functools.partial(kernel, n_sp, n_grp, n_core, part_rows),
        out_shape=(
            jax.ShapeDtypeStruct(cotangent.shape, bf16),
            jax.ShapeDtypeStruct(acts.shape, bf16),
            jax.ShapeDtypeStruct((width, channels), f32),
        ),
        in_specs=[anywhere, anywhere, in_vmem, anywhere, in_vmem, in_vmem],
        out_specs=(in_vmem, in_vmem, in_vmem),
        scratch_shapes=[
            vmem((n_rows, n_samples, cols, channels), bf16),
            vmem((n_samples, n_rows, cols, channels), bf16),
            vmem((channels, channels), bf16),
            vmem((n_rows * rows, channels), bf16),
            vmem((n_rows, rows, channels), f32),
            vmem((n_rows + 2, rows, channels), bf16),
            vmem((n_grp * part_rows, n_rows * rows), bf16),
            vmem((3, rows, channels), f32),
            vmem((n_z, part_rows, channels), bf16),
            vmem((n_z, part_rows, channels), bf16),
            vmem((n_z, part_rows, channels), f32),
            vmem((n_z, part_rows, channels), bf16),
            vmem((n_z, part_rows, channels), bf16),
            vmem((n_core, n_z, part_rows, channels), bf16),
            dma((3,)),
            dma((n_sp,)), dma((n_sp,)), dma((n_sp,)), dma((n_sp,)),
            dma((n_z,)), dma((n_z,)), dma((n_z,)), dma((n_z,)),
            dma((n_z,)), dma((n_z,)), dma((n_z,)), dma((n_z,)),
        ],
        compiler_params=pltpu.CompilerParams(collective_id=0, has_side_effects=True),
        name="middle_flow",
    )(acts, cotangent, depth_kernel, point_weight, gain.reshape(1, -1), bias.reshape(1, -1))
    return out[0], out[1], out[2].reshape(-1)


def depth_forward(field, filter_weight):
    rows = field.shape[1]
    cols = field.shape[2]
    padded = jnp.pad(field, ((0, 0), (1, 1), (1, 1), (0, 0)))
    total = jnp.zeros(field.shape, jnp.float32)
    for i in range(3):
        for j in range(3):
            total = total + padded[:, i : i + rows, j : j + cols, :] * filter_weight[i, j]
    return total


def depth_backward(field, filter_weight):
    rows = field.shape[1]
    cols = field.shape[2]
    padded = jnp.pad(field, ((0, 0), (1, 1), (1, 1), (0, 0)))
    total = jnp.zeros(field.shape, jnp.float32)
    for i in range(3):
        for j in range(3):
            total = (
                total
                + padded[:, 2 - i : 2 - i + rows, 2 - j : 2 - j + cols, :] * filter_weight[i, j]
            )
    return total


def body(acts, cotangent, depth_kernel, point_weight, batch_norm_gain, norm_shift_bias):
    channel_count = acts.shape[-1]
    sample_image = lax.all_to_all(acts, "sp", split_axis=0, concat_axis=1, tiled=True)
    input_single_precision = sample_image.astype(jnp.float32)
    hidden = jnp.maximum(input_single_precision, 0.0)
    depthed = depth_forward(hidden, depth_kernel).astype(jnp.bfloat16)
    flat_d = depthed.reshape(-1, channel_count)
    element_count = flat_d.shape[0] * lax.axis_size("sp")
    projected_output = jnp.dot(flat_d, point_weight, preferred_element_type=jnp.float32)
    total, squares = lax.psum(
        (jnp.sum(projected_output, axis=0), jnp.sum(projected_output * projected_output, axis=0)),
        "sp",
    )
    batch_mean = total / element_count
    var = squares / element_count - batch_mean * batch_mean
    inverse_deviation = lax.rsqrt(var + 1e-05)
    normalized_input = (projected_output - batch_mean) * inverse_deviation
    block_out = (
        (
            input_single_precision.reshape(-1, channel_count)
            + batch_norm_gain * normalized_input
            + norm_shift_bias
        )
        .astype(jnp.bfloat16)
        .reshape(sample_image.shape)
    )
    gfloat = cotangent.astype(jnp.float32).reshape(-1, channel_count)
    scaled_output = gfloat * batch_norm_gain
    leading_layer, second_layer = lax.psum(
        (jnp.sum(scaled_output, axis=0), jnp.sum(scaled_output * normalized_input, axis=0)), "sp"
    )
    projected_gradient = (
        inverse_deviation
        * (
            scaled_output
            - leading_layer / element_count
            - normalized_input * (second_layer / element_count)
        )
    ).astype(jnp.bfloat16)
    local_weight = jnp.dot(
        flat_d.T, projected_gradient, preferred_element_type=jnp.float32
    ).reshape(-1)
    ddepth = jnp.dot(
        projected_gradient, point_weight.T, preferred_element_type=jnp.float32
    ).reshape(sample_image.shape)
    dhidden = depth_backward(ddepth, depth_kernel)
    dinput = (
        gfloat.reshape(sample_image.shape) + jnp.where(sample_image > 0, dhidden, 0.0)
    ).astype(jnp.bfloat16)
    input_grad = lax.all_to_all(dinput, "sp", split_axis=1, concat_axis=0, tiled=True)
    slices = lax.psum_scatter(
        local_weight.astype(jnp.bfloat16), "sp", scatter_dimension=0, tiled=True
    ).astype(jnp.float32)
    weight_grad = lax.psum(slices, "grp")
    return (block_out, input_grad, weight_grad)


def one_kernel_fits(mesh, acts, cotangent):
    n_sp, n_grp = mesh.shape["sp"], mesh.shape["grp"]
    group_elements = acts.size // n_grp
    return (
        acts.shape[1] == n_sp
        and acts.shape[0] == n_sp * n_grp
        and acts.shape[2] % 16 == 0
        and acts.shape[3] % n_sp == 0
        and n_grp % 2 == 0
        and n_grp > 2
        and n_sp > 1
        and group_elements <= 1 << 20
    )


def solution(mesh):
    in_specs = (P("grp", "sp", None, None), P(("grp", "sp"), None, None, None), P(), P(), P(), P())
    out_specs = (P(("grp", "sp"), None, None, None), P("grp", "sp", None, None), P("sp"))

    def step(acts, cotangent, *params):
        inner = fused if one_kernel_fits(mesh, acts, cotangent) else body
        mapped = jax.shard_map(
            inner, mesh=mesh, in_specs=in_specs, out_specs=out_specs, check_vma=False
        )
        return mapped(acts, cotangent, *params)

    return step
```

```python
import functools

import jax
import jax.numpy as jnp
from jax import lax
from jax.experimental import pallas as pl
from jax.experimental.pallas import tpu as pltpu
from jax.sharding import PartitionSpec as P

MESH = pl.DeviceIdType.MESH
LANES = 128
NT = (((1,), (1,)), ((), ()))


def lane_blocks(channels):
    return [slice(at, min(at + LANES, channels)) for at in range(0, channels, LANES)]


def column_shift(field, step):
    cols = field.shape[0]
    at = lax.broadcasted_iota(jnp.int32, field.shape, 0)
    keep = (at >= 1) if step > 0 else (at < cols - 1)
    return jnp.where(keep, pltpu.roll(field, step % cols, 0), 0.0)


def kernel(
    n_sp, n_grp, n_core, n_parts, part_rows,
    acts_ref, cot_ref, dk_ref, pw_hbm, gain_ref, bias_ref,
    block_out_ref, input_grad_ref, weight_ref,
    ga, gc, pw, d_ref, p_ref, dp_ref, dsel_ref, dd_ref,
    pair_send, pair_recv, own_ref, z_send, z_recv, res_ref,
    local_sem, a_send, a_recv, c_send, c_recv,
    pair_ssem, pair_rsem, z_ssem, z_rsem, g_ssem, g_rsem, f_ssem, f_rsem,
):
    sp = lax.axis_index("sp")
    grp = lax.axis_index("grp")
    n_z = n_grp // n_core
    z, core = grp // n_core, grp % n_core
    other = (core + 1) % n_core
    partner = z * n_core + other
    middle = n_z // 2
    toward = z + 1 - 2 * (z // middle)
    away = 2 * z - toward
    across = (toward // middle - z // middle) * (toward // middle - z // middle)
    inner = (z > 0) & (z < n_z - 1)
    side = int(n_sp**0.5)
    sx = (sp // side) * side + (sp + 1) % side
    sy = (sp + side) % n_sp
    far = (sx + side) % n_sp
    n_rows, n_samples, cols, channels = ga.shape
    count = n_rows * n_samples * cols
    blocks = lane_blocks(channels)

    load_pw = pltpu.make_async_copy(pw_hbm, pw, local_sem.at[0])
    load_pw.start()
    own_acts = pltpu.make_async_copy(acts_ref.at[:, 0], ga.at[sp], local_sem.at[1])
    own_acts.start()
    own_cot = pltpu.make_async_copy(cot_ref.at[0], gc.at[sp], local_sem.at[2])
    own_cot.start()

    barrier = pltpu.get_barrier_semaphore()

    def greet(peer):
        pl.semaphore_signal(barrier, inc=1, device_id=peer, device_id_type=MESH)

    def z_core(at):
        return {"grp": at * n_core + core}

    peers = [{"sp": sx}, {"sp": sy}, {"grp": partner}, z_core(toward)]
    for peer in peers:
        greet(peer)

    @pl.when(inner)
    def _():
        greet(z_core(away))
        pl.semaphore_wait(barrier, len(peers) + 1)

    @pl.when(jnp.logical_not(inner))
    def _():
        pl.semaphore_wait(barrier, len(peers))

    class Gather:
        def __init__(self, own, buf, send, recv):
            self.own, self.buf, self.send, self.recv = own, buf, send, recv
            self.size = buf.shape[1] // 2

        def part(self, half):
            return pl.ds(half * self.size, self.size)

        def copy(self, k, src, slot, half, to):
            return pltpu.make_async_remote_copy(
                src_ref=src, dst_ref=self.buf.at[slot, self.part(half)],
                send_sem=self.send.at[k], recv_sem=self.recv.at[slot, half],
                device_id={"sp": to}, device_id_type=MESH,
            )

        def direct(self):
            return [
                self.copy(k, self.own.at[self.part(half)], sp, half, to)
                for k, (half, to) in enumerate(((0, sx), (1, sy), (1, sx), (0, sy)))
            ]

        def relays(self):
            return [
                self.copy(4, self.buf.at[sx, self.part(0)], sx, 0, sy),
                self.copy(5, self.buf.at[sy, self.part(1)], sy, 1, sx),
            ]

        def arrived(self, slot, half):
            self.copy(0, self.buf.at[slot, self.part(half)], slot, half, sx).wait_recv()

        def start(self):
            for copy in self.direct():
                copy.start()

        def relay(self):
            for copy, slot, half in zip(self.relays(), (sx, sy), (0, 1)):
                self.arrived(slot, half)
                copy.start()

        def finish(self):
            for slot, half in ((sx, 1), (sy, 0), (far, 0), (far, 1)):
                self.arrived(slot, half)

        def sent(self):
            for copy in self.direct() + self.relays():
                copy.wait_send()

    acts_gather = Gather(acts_ref.at[:, 0], ga, a_send, a_recv)
    cot_gather = Gather(cot_ref.at[0], gc, c_send, c_recv)
    acts_gather.start()
    dp_ref[0] = jnp.zeros(dp_ref.shape[1:], dp_ref.dtype)
    dp_ref[n_rows + 1] = jnp.zeros(dp_ref.shape[1:], dp_ref.dtype)
    acts_gather.relay()
    cot_gather.start()
    own_acts.wait()
    load_pw.wait()
    acts_gather.finish()

    @pl.loop(0, n_samples)
    def _(b):
        for lanes in blocks:
            h = [jnp.maximum(ga[r, b, :, lanes].astype(jnp.float32), 0.0) for r in range(n_rows)]
            taps = [[dk_ref[i, j : j + 1, lanes] for j in range(3)] for i in range(3)]
            for r in range(n_rows):
                t = [
                    sum(h[r + i - 1] * taps[i][j] for i in range(3) if 0 <= r + i - 1 < n_rows)
                    for j in range(3)
                ]
                total = t[1] + column_shift(t[0], 1) + column_shift(t[2], -1)
                at = pl.multiple_of((r * n_samples + b) * cols, cols)
                d_ref[pl.ds(at, cols), lanes] = total.astype(jnp.bfloat16)

    cot_gather.relay()
    p_ref[...] = jnp.dot(
        d_ref[...], pw[...], preferred_element_type=jnp.float32
    ).reshape(p_ref.shape)
    sel_rows = dsel_ref.shape[0]
    width = channels // n_sp
    row = lax.broadcasted_iota(jnp.int32, (sel_rows, channels), 0)
    lane = lax.broadcasted_iota(jnp.int32, (sel_rows, channels), 1)
    pick = jnp.where((lane - sp * width == row) & (row < width), 1.0, 0.0).astype(jnp.bfloat16)
    dsel_ref[...] = lax.dot_general(
        pick, d_ref[...], NT, preferred_element_type=jnp.float32
    ).astype(jnp.bfloat16)

    own_cot.wait()
    cot_gather.finish()

    means, rstds = [], []
    for lanes in blocks:
        size = lanes.stop - lanes.start
        s1 = s2 = sg = sgp = jnp.zeros((cols, size), jnp.float32)
        for r in range(n_rows):
            for b in range(n_samples):
                p = p_ref[r, b * cols : (b + 1) * cols, lanes]
                g = gc[b, r, :, lanes].astype(jnp.float32)
                s1, s2, sg, sgp = s1 + p, s2 + p * p, sg + g, sgp + g * p
        s1, s2, sg, sgp = [jnp.sum(s, axis=0, keepdims=True) for s in (s1, s2, sg, sgp)]
        gain = gain_ref[lanes].reshape(1, -1)
        mean = s1 / count
        var = s2 / count - mean * mean
        rstd = lax.rsqrt(var + 1e-05)
        a1 = gain * sg / count
        a2 = gain * rstd * (sgp - mean * sg) / count
        means.append(mean)
        rstds.append(rstd)
        for r in range(n_rows):
            for b in range(n_samples):
                p = p_ref[r, b * cols : (b + 1) * cols, lanes]
                g = gc[b, r, :, lanes].astype(jnp.float32)
                xhat = (p - mean) * rstd
                dp_ref[r + 1, b * cols : (b + 1) * cols, lanes] = (
                    rstd * (g * gain - a1 - xhat * a2)
                ).astype(jnp.bfloat16)

    half = n_parts * part_rows

    def product(which):
        left = dsel_ref[pl.ds(pl.multiple_of(which * half, half), half), :]
        return jnp.dot(
            left, dp_ref[1 : n_rows + 1].reshape(-1, channels), preferred_element_type=jnp.float32
        ).reshape(n_parts, part_rows, channels)

    def pair_copy(k):
        return pltpu.make_async_remote_copy(
            src_ref=pair_send.at[k], dst_ref=pair_recv.at[k],
            send_sem=pair_ssem.at[k], recv_sem=pair_rsem.at[k],
            device_id={"grp": partner}, device_id_type=MESH,
        )

    def in_copy(k, slot):
        return pltpu.make_async_remote_copy(
            src_ref=z_send.at[k], dst_ref=z_recv.at[slot, k],
            send_sem=z_ssem.at[k], recv_sem=z_rsem.at[slot, k],
            device_id=z_core(toward), device_id_type=MESH,
        )

    def out_copy(k):
        return pltpu.make_async_remote_copy(
            src_ref=res_ref.at[core, k], dst_ref=res_ref.at[core, k],
            send_sem=g_ssem.at[k], recv_sem=g_rsem.at[k],
            device_id=z_core(away), device_id_type=MESH,
        )

    def forward_copy(k, owner):
        return pltpu.make_async_remote_copy(
            src_ref=res_ref.at[owner, k], dst_ref=res_ref.at[owner, k],
            send_sem=f_ssem.at[k], recv_sem=f_rsem.at[k],
            device_id={"grp": partner}, device_id_type=MESH,
        )

    pair_send[...] = product(other).astype(jnp.bfloat16)
    for k in range(n_parts):
        pair_copy(k).start()
    own_ref[...] = product(core)
    dd_ref[...] = lax.dot_general(
        dp_ref[pl.ds(sp, 3)].reshape(-1, channels), pw[...], NT,
        preferred_element_type=jnp.float32,
    ).reshape(dd_ref.shape)

    def reduce_in(k):
        pair_copy(k).wait_recv()
        own_ref[k] += pair_recv[k].astype(jnp.float32)

        @pl.when(inner)
        def _():
            in_copy(k, 0).wait_recv()
            own_ref[k] += z_recv[0, k].astype(jnp.float32)

        z_send[k] = own_ref[k].astype(jnp.bfloat16)
        in_copy(k, across).start()

    def spread_out(k):
        @pl.when(across == 1)
        def _():
            in_copy(k, 1).wait_recv()
            total = z_send[k].astype(jnp.float32) + z_recv[1, k].astype(jnp.float32)
            res_ref[core, k] = total.astype(jnp.bfloat16)

        @pl.when(across == 0)
        def _():
            out_copy(k).wait_recv()

        @pl.when(inner)
        def _():
            out_copy(k).start()

        forward_copy(k, core).start()

    def outputs(at):
        lanes = blocks[at]
        taps = [[dk_ref[i, j : j + 1, lanes] for j in range(3)] for i in range(3)]
        gain, bias = gain_ref[lanes].reshape(1, -1), bias_ref[lanes].reshape(1, -1)
        for b in range(n_samples):
            own = slice(b * cols, (b + 1) * cols)
            dd = [dd_ref[i, own, lanes] for i in range(3)]
            t = [sum(dd[2 - i] * taps[i][j] for i in range(3)) for j in range(3)]
            dh = t[1] + column_shift(t[0], -1) + column_shift(t[2], 1)
            a = ga[sp, b, :, lanes].astype(jnp.float32)
            g = gc[b, sp, :, lanes].astype(jnp.float32)
            input_grad_ref[b, 0, :, lanes] = (g + jnp.where(a > 0, dh, 0.0)).astype(jnp.bfloat16)
        for r in range(n_rows):
            p = p_ref[r, pl.ds(pl.multiple_of(sp * cols, cols), cols), lanes]
            a = ga[r, sp, :, lanes].astype(jnp.float32)
            block_out_ref[0, r, :, lanes] = (
                a + gain * ((p - means[at]) * rstds[at]) + bias
            ).astype(jnp.bfloat16)

    lag = 2
    for k in range(n_parts + lag):
        if k < n_parts:
            reduce_in(k)
        for at in range(k, len(blocks), n_parts):
            if k < n_parts:
                outputs(at)
        if k >= lag:
            spread_out(k - lag)

    def write(owner, k):
        at = (owner * n_parts + k) * part_rows
        size = min(part_rows, width - at)
        weight_ref[at : at + size] = res_ref[owner, k, :size].astype(jnp.float32)

    for k in range(n_parts):
        forward_copy(k, other).wait_recv()
    for owner in range(n_core):
        for k in range(n_parts):
            write(owner, k)

    acts_gather.sent()
    cot_gather.sent()
    for k in range(n_parts):
        pair_copy(k).wait_send()
        in_copy(k, across).wait_send()
        forward_copy(k, core).wait_send()

        @pl.when(inner)
        def _():
            out_copy(k).wait_send()


def fused(acts, cotangent, depth_kernel, point_weight, gain, bias):
    n_sp, n_grp, n_core = lax.axis_size("sp"), lax.axis_size("grp"), 2
    n_samples, _, cols, channels = acts.shape
    n_rows = cotangent.shape[1]
    n_parts = 4
    width = channels // n_sp
    part_rows = -(-width // (n_core * n_parts * 8)) * 8
    bf16, f32 = jnp.bfloat16, jnp.float32
    vmem, dma = pltpu.VMEM, pltpu.SemaphoreType.DMA
    in_vmem, anywhere = pl.BlockSpec(memory_space=pltpu.VMEM), pl.BlockSpec(memory_space=pl.ANY)
    rows = n_samples * cols
    out = pl.pallas_call(
        functools.partial(kernel, n_sp, n_grp, n_core, n_parts, part_rows),
        out_shape=(
            jax.ShapeDtypeStruct(cotangent.shape, bf16),
            jax.ShapeDtypeStruct(acts.shape, bf16),
            jax.ShapeDtypeStruct((width, channels), f32),
        ),
        in_specs=[anywhere, anywhere, in_vmem, anywhere, in_vmem, in_vmem],
        out_specs=(in_vmem, in_vmem, in_vmem),
        scratch_shapes=[
            vmem((n_rows, n_samples, cols, channels), bf16),
            vmem((n_samples, n_rows, cols, channels), bf16),
            vmem((channels, channels), bf16),
            vmem((n_rows * rows, channels), bf16),
            vmem((n_rows, rows, channels), f32),
            vmem((n_rows + 2, rows, channels), bf16),
            vmem((n_core * n_parts * part_rows, n_rows * rows), bf16),
            vmem((3, rows, channels), f32),
            vmem((n_parts, part_rows, channels), bf16),
            vmem((n_parts, part_rows, channels), bf16),
            vmem((n_parts, part_rows, channels), f32),
            vmem((n_parts, part_rows, channels), bf16),
            vmem((2, n_parts, part_rows, channels), bf16),
            vmem((n_core, n_parts, part_rows, channels), bf16),
            dma((3,)),
            dma((6,)), dma((n_sp, 2)), dma((6,)), dma((n_sp, 2)),
            dma((n_parts,)), dma((n_parts,)), dma((n_parts,)), dma((2, n_parts)),
            dma((n_parts,)), dma((n_parts,)), dma((n_parts,)), dma((n_parts,)),
        ],
        compiler_params=pltpu.CompilerParams(collective_id=0, has_side_effects=True),
        name="middle_flow",
    )(acts, cotangent, depth_kernel, point_weight, gain, bias)
    return out[0], out[1], out[2].reshape(-1)


def depth_forward(field, filter_weight):
    rows = field.shape[1]
    cols = field.shape[2]
    padded = jnp.pad(field, ((0, 0), (1, 1), (1, 1), (0, 0)))
    total = jnp.zeros(field.shape, jnp.float32)
    for i in range(3):
        for j in range(3):
            total = total + padded[:, i : i + rows, j : j + cols, :] * filter_weight[i, j]
    return total


def depth_backward(field, filter_weight):
    rows = field.shape[1]
    cols = field.shape[2]
    padded = jnp.pad(field, ((0, 0), (1, 1), (1, 1), (0, 0)))
    total = jnp.zeros(field.shape, jnp.float32)
    for i in range(3):
        for j in range(3):
            total = (
                total
                + padded[:, 2 - i : 2 - i + rows, 2 - j : 2 - j + cols, :] * filter_weight[i, j]
            )
    return total


def body(acts, cotangent, depth_kernel, point_weight, batch_norm_gain, norm_shift_bias):
    channel_count = acts.shape[-1]
    sample_image = lax.all_to_all(acts, "sp", split_axis=0, concat_axis=1, tiled=True)
    input_single_precision = sample_image.astype(jnp.float32)
    hidden = jnp.maximum(input_single_precision, 0.0)
    depthed = depth_forward(hidden, depth_kernel).astype(jnp.bfloat16)
    flat_d = depthed.reshape(-1, channel_count)
    element_count = flat_d.shape[0] * lax.axis_size("sp")
    projected_output = jnp.dot(flat_d, point_weight, preferred_element_type=jnp.float32)
    total, squares = lax.psum(
        (jnp.sum(projected_output, axis=0), jnp.sum(projected_output * projected_output, axis=0)),
        "sp",
    )
    batch_mean = total / element_count
    var = squares / element_count - batch_mean * batch_mean
    inverse_deviation = lax.rsqrt(var + 1e-05)
    normalized_input = (projected_output - batch_mean) * inverse_deviation
    block_out = (
        (
            input_single_precision.reshape(-1, channel_count)
            + batch_norm_gain * normalized_input
            + norm_shift_bias
        )
        .astype(jnp.bfloat16)
        .reshape(sample_image.shape)
    )
    gfloat = cotangent.astype(jnp.float32).reshape(-1, channel_count)
    scaled_output = gfloat * batch_norm_gain
    leading_layer, second_layer = lax.psum(
        (jnp.sum(scaled_output, axis=0), jnp.sum(scaled_output * normalized_input, axis=0)), "sp"
    )
    projected_gradient = (
        inverse_deviation
        * (
            scaled_output
            - leading_layer / element_count
            - normalized_input * (second_layer / element_count)
        )
    ).astype(jnp.bfloat16)
    local_weight = jnp.dot(
        flat_d.T, projected_gradient, preferred_element_type=jnp.float32
    ).reshape(-1)
    ddepth = jnp.dot(
        projected_gradient, point_weight.T, preferred_element_type=jnp.float32
    ).reshape(sample_image.shape)
    dhidden = depth_backward(ddepth, depth_kernel)
    dinput = (
        gfloat.reshape(sample_image.shape) + jnp.where(sample_image > 0, dhidden, 0.0)
    ).astype(jnp.bfloat16)
    input_grad = lax.all_to_all(dinput, "sp", split_axis=1, concat_axis=0, tiled=True)
    slices = lax.psum_scatter(
        local_weight.astype(jnp.bfloat16), "sp", scatter_dimension=0, tiled=True
    ).astype(jnp.float32)
    weight_grad = lax.psum(slices, "grp")
    return (block_out, input_grad, weight_grad)


def one_kernel_fits(mesh, acts, cotangent):
    n_sp, n_grp = mesh.shape["sp"], mesh.shape["grp"]
    group_elements = acts.size // n_grp
    return (
        acts.shape[1] == n_sp
        and acts.shape[0] == n_sp * n_grp
        and acts.shape[2] % 16 == 0
        and acts.shape[3] % n_sp == 0
        and n_grp % 4 == 0
        and n_sp == 4
        and group_elements <= 1 << 20
    )


def solution(mesh):
    in_specs = (P("grp", "sp", None, None), P(("grp", "sp"), None, None, None), P(), P(), P(), P())
    out_specs = (P(("grp", "sp"), None, None, None), P("grp", "sp", None, None), P("sp"))

    def step(acts, cotangent, *params):
        inner = fused if one_kernel_fits(mesh, acts, cotangent) else body
        mapped = jax.shard_map(
            inner, mesh=mesh, in_specs=in_specs, out_specs=out_specs, check_vma=False
        )
        return mapped(acts, cotangent, *params)

    return step
```

```python
import functools

import jax
import jax.numpy as jnp
from jax import lax
from jax.experimental import pallas as pl
from jax.experimental.pallas import tpu as pltpu
from jax.sharding import PartitionSpec as P

MESH = pl.DeviceIdType.MESH
LANES = 128
NT = (((1,), (1,)), ((), ()))


def lane_blocks(channels):
    return [slice(at, min(at + LANES, channels)) for at in range(0, channels, LANES)]


def column_shift(field, step):
    cols = field.shape[0]
    at = lax.broadcasted_iota(jnp.int32, field.shape, 0)
    keep = (at >= 1) if step > 0 else (at < cols - 1)
    return jnp.where(keep, pltpu.roll(field, step % cols, 0), 0.0)


def kernel(
    n_sp, n_grp, n_core, n_parts, part_rows,
    acts_ref, cot_ref, dk_ref, pw_hbm, gain_ref, bias_ref,
    block_out_ref, input_grad_ref, weight_ref,
    ga, gc, pw, d_ref, p_ref, dp_ref, dsel_ref, dd_ref,
    pair_send, pair_recv, own_ref, z_send, z_recv, res_ref,
    local_sem, ready, a_send, a_recv, c_send, c_recv,
    pair_ssem, pair_rsem, z_ssem, z_rsem, g_ssem, g_rsem, f_ssem, f_rsem,
):
    sp = lax.axis_index("sp")
    grp = lax.axis_index("grp")
    n_z = n_grp // n_core
    z, core = grp // n_core, grp % n_core
    other = (core + 1) % n_core
    partner = z * n_core + other
    middle = n_z // 2
    toward = z + 1 - 2 * (z // middle)
    away = 2 * z - toward
    inner = (z > 0) & (z < n_z - 1)
    side = int(n_sp**0.5)
    sx = (sp // side) * side + (sp + 1) % side
    sy = (sp + side) % n_sp
    far = (sx + side) % n_sp
    n_rows, n_samples, cols, channels = ga.shape
    count = n_rows * n_samples * cols
    blocks = lane_blocks(channels)

    load_pw = pltpu.make_async_copy(pw_hbm, pw, local_sem.at[0])
    load_pw.start()
    own_acts = pltpu.make_async_copy(acts_ref.at[:, 0], ga.at[sp], local_sem.at[1])
    own_acts.start()
    own_cot = pltpu.make_async_copy(cot_ref.at[0], gc.at[sp], local_sem.at[2])
    own_cot.start()

    barrier = pltpu.get_barrier_semaphore()

    def greet(peer):
        pl.semaphore_signal(barrier, inc=1, device_id=peer, device_id_type=MESH)

    def z_core(at):
        return {"grp": at * n_core + core}

    peers = [{"sp": sx}, {"sp": sy}, {"grp": partner}, z_core(toward)]
    for peer in peers:
        greet(peer)

    @pl.when(inner)
    def _():
        greet(z_core(away))
        pl.semaphore_wait(barrier, len(peers) + 1)

    @pl.when(jnp.logical_not(inner))
    def _():
        pl.semaphore_wait(barrier, len(peers))

    class Gather:
        def __init__(self, own, buf, send, recv):
            self.own, self.buf, self.send, self.recv = own, buf, send, recv
            self.size = buf.shape[1] // 2

        def part(self, half):
            return pl.ds(half * self.size, self.size)

        def copy(self, k, src, slot, half, to):
            return pltpu.make_async_remote_copy(
                src_ref=src, dst_ref=self.buf.at[slot, self.part(half)],
                send_sem=self.send.at[k], recv_sem=self.recv.at[slot, half],
                device_id={"sp": to}, device_id_type=MESH,
            )

        def direct(self):
            return [
                self.copy(k, self.own.at[self.part(half)], sp, half, to)
                for k, (half, to) in enumerate(((0, sx), (1, sy), (1, sx), (0, sy)))
            ]

        def start_relayed(self):
            for copy in self.direct()[:2]:
                copy.start()

        def start_rest(self):
            for copy in self.direct()[2:]:
                copy.start()

        def relays(self):
            return [
                self.copy(4, self.buf.at[sx, self.part(0)], sx, 0, sy),
                self.copy(5, self.buf.at[sy, self.part(1)], sy, 1, sx),
            ]

        def arrived(self, slot, half):
            self.copy(0, self.buf.at[slot, self.part(half)], slot, half, sx).wait_recv()

        def relay(self):
            for copy, slot, half in zip(self.relays(), (sx, sy), (0, 1)):
                self.arrived(slot, half)
                copy.start()

        def finish(self):
            for slot, half in ((sx, 1), (sy, 0), (far, 0), (far, 1)):
                self.arrived(slot, half)

        def sent(self):
            for copy in self.direct() + self.relays():
                copy.wait_send()

    acts_gather = Gather(acts_ref.at[:, 0], ga, a_send, a_recv)
    cot_gather = Gather(cot_ref.at[0], gc, c_send, c_recv)
    acts_gather.start_relayed()
    acts_gather.start_rest()
    cot_gather.start_relayed()
    dp_ref[0] = jnp.zeros(dp_ref.shape[1:], dp_ref.dtype)
    dp_ref[n_rows + 1] = jnp.zeros(dp_ref.shape[1:], dp_ref.dtype)
    acts_gather.relay()
    cot_gather.start_rest()
    for level in range(n_z - 2):
        for step in (1, -1):
            there = (z + step >= 0) & (z + step < n_z)

            @pl.when(there)
            def _():
                pl.semaphore_signal(
                    ready.at[level, (1 - step) // 2], inc=1,
                    device_id=z_core(z + step), device_id_type=MESH,
                )

        for step in (1, -1):
            there = (z + step >= 0) & (z + step < n_z)

            @pl.when(there)
            def _():
                pl.semaphore_wait(ready.at[level, (1 + step) // 2], 1)

    own_acts.wait()
    load_pw.wait()
    cot_gather.relay()
    acts_gather.finish()

    @pl.loop(0, n_samples)
    def _(b):
        for lanes in blocks:
            h = [jnp.maximum(ga[r, b, :, lanes].astype(jnp.float32), 0.0) for r in range(n_rows)]
            taps = [[dk_ref[i, j : j + 1, lanes] for j in range(3)] for i in range(3)]
            for r in range(n_rows):
                t = [
                    sum(h[r + i - 1] * taps[i][j] for i in range(3) if 0 <= r + i - 1 < n_rows)
                    for j in range(3)
                ]
                total = t[1] + column_shift(t[0], 1) + column_shift(t[2], -1)
                at = pl.multiple_of((r * n_samples + b) * cols, cols)
                d_ref[pl.ds(at, cols), lanes] = total.astype(jnp.bfloat16)

    p_ref[...] = jnp.dot(
        d_ref[...], pw[...], preferred_element_type=jnp.float32
    ).reshape(p_ref.shape)
    sel_rows = dsel_ref.shape[0]
    width = channels // n_sp
    row = lax.broadcasted_iota(jnp.int32, (sel_rows, channels), 0)
    lane = lax.broadcasted_iota(jnp.int32, (sel_rows, channels), 1)
    pick = jnp.where((lane - sp * width == row) & (row < width), 1.0, 0.0).astype(jnp.bfloat16)
    dsel_ref[...] = lax.dot_general(
        pick, d_ref[...], NT, preferred_element_type=jnp.float32
    ).astype(jnp.bfloat16)

    own_cot.wait()
    cot_gather.finish()

    means, rstds = [], []
    for lanes in blocks:
        size = lanes.stop - lanes.start
        s1 = s2 = sg = sgp = jnp.zeros((cols, size), jnp.float32)
        for r in range(n_rows):
            for b in range(n_samples):
                p = p_ref[r, b * cols : (b + 1) * cols, lanes]
                g = gc[b, r, :, lanes].astype(jnp.float32)
                s1, s2, sg, sgp = s1 + p, s2 + p * p, sg + g, sgp + g * p
        s1, s2, sg, sgp = [jnp.sum(s, axis=0, keepdims=True) for s in (s1, s2, sg, sgp)]
        gain = gain_ref[lanes].reshape(1, -1)
        mean = s1 / count
        var = s2 / count - mean * mean
        rstd = lax.rsqrt(var + 1e-05)
        a1 = gain * sg / count
        a2 = gain * rstd * (sgp - mean * sg) / count
        means.append(mean)
        rstds.append(rstd)
        for r in range(n_rows):
            for b in range(n_samples):
                p = p_ref[r, b * cols : (b + 1) * cols, lanes]
                g = gc[b, r, :, lanes].astype(jnp.float32)
                xhat = (p - mean) * rstd
                dp_ref[r + 1, b * cols : (b + 1) * cols, lanes] = (
                    rstd * (g * gain - a1 - xhat * a2)
                ).astype(jnp.bfloat16)

    half = n_parts * part_rows

    def product(which):
        left = dsel_ref[pl.ds(pl.multiple_of(which * half, half), half), :]
        return jnp.dot(
            left, dp_ref[1 : n_rows + 1].reshape(-1, channels), preferred_element_type=jnp.float32
        ).reshape(n_parts, part_rows, channels)

    def pair_copy(k):
        return pltpu.make_async_remote_copy(
            src_ref=pair_send.at[k], dst_ref=pair_recv.at[k],
            send_sem=pair_ssem.at[k], recv_sem=pair_rsem.at[k],
            device_id={"grp": partner}, device_id_type=MESH,
        )

    def z_copy(k, slot, to):
        return pltpu.make_async_remote_copy(
            src_ref=z_send.at[k], dst_ref=z_recv.at[slot],
            send_sem=z_ssem.at[k], recv_sem=z_rsem.at[slot],
            device_id=z_core(to), device_id_type=MESH,
        )

    def gather_copy(k, slot, to):
        return pltpu.make_async_remote_copy(
            src_ref=res_ref.at[core, slot], dst_ref=res_ref.at[core, slot],
            send_sem=g_ssem.at[k], recv_sem=g_rsem.at[slot],
            device_id=z_core(to), device_id_type=MESH,
        )

    def forward_copy(k, owner):
        return pltpu.make_async_remote_copy(
            src_ref=res_ref.at[owner, k], dst_ref=res_ref.at[owner, k],
            send_sem=f_ssem.at[k], recv_sem=f_rsem.at[k],
            device_id={"grp": partner}, device_id_type=MESH,
        )

    def outputs(at):
        lanes = blocks[at]
        taps = [[dk_ref[i, j : j + 1, lanes] for j in range(3)] for i in range(3)]
        gain, bias = gain_ref[lanes].reshape(1, -1), bias_ref[lanes].reshape(1, -1)
        for b in range(n_samples):
            own = slice(b * cols, (b + 1) * cols)
            dd = [dd_ref[i, own, lanes] for i in range(3)]
            t = [sum(dd[2 - i] * taps[i][j] for i in range(3)) for j in range(3)]
            dh = t[1] + column_shift(t[0], -1) + column_shift(t[2], 1)
            a = ga[sp, b, :, lanes].astype(jnp.float32)
            g = gc[b, sp, :, lanes].astype(jnp.float32)
            input_grad_ref[b, 0, :, lanes] = (g + jnp.where(a > 0, dh, 0.0)).astype(jnp.bfloat16)
        for r in range(n_rows):
            p = p_ref[r, pl.ds(pl.multiple_of(sp * cols, cols), cols), lanes]
            a = ga[r, sp, :, lanes].astype(jnp.float32)
            block_out_ref[0, r, :, lanes] = (
                a + gain * ((p - means[at]) * rstds[at]) + bias
            ).astype(jnp.bfloat16)

    def write(owner, k):
        at = (owner * n_parts + k) * part_rows
        size = min(part_rows, width - at)
        weight_ref[at : at + size] = res_ref[owner, k, :size].astype(jnp.float32)

    pair_send[...] = product(other).astype(jnp.bfloat16)
    for k in range(1, n_z + 1):
        pair_copy((z + k) % n_z).start()
    own_ref[...] = product(core)
    for k in range(1, n_z):
        to = (z + k) % n_z
        pair_copy(to).wait_recv()
        z_send[to] = (own_ref[to] + pair_recv[to].astype(jnp.float32)).astype(jnp.bfloat16)
        z_copy(to, z, to).start()

    dd_ref[...] = lax.dot_general(
        dp_ref[pl.ds(sp, 3)].reshape(-1, channels), pw[...], NT,
        preferred_element_type=jnp.float32,
    ).reshape(dd_ref.shape)

    pair_copy(z).wait_recv()
    mine = own_ref[z] + pair_recv[z].astype(jnp.float32)
    for k in range(1, n_z):
        slot = (z + k) % n_z
        z_copy(slot, slot, z).wait_recv()
        mine = mine + z_recv[slot].astype(jnp.float32)
    res_ref[core, z] = mine.astype(jnp.bfloat16)
    for k in range(1, n_z):
        gather_copy(k, z, (z + k) % n_z).start()
    forward_copy(z, core).start()

    for at in range(len(blocks)):
        outputs(at)

    for k in range(1, n_z):
        slot = (z + k) % n_z
        gather_copy(k, slot, z).wait_recv()
        forward_copy(slot, core).start()
    for k in range(n_z):
        forward_copy((z + k) % n_z, other).wait_recv()
    for owner in range(n_core):
        for k in range(n_z):
            write(owner, k)

    acts_gather.sent()
    cot_gather.sent()
    for k in range(n_z):
        pair_copy(k).wait_send()
        forward_copy(k, core).wait_send()
    for k in range(1, n_z):
        z_copy((z + k) % n_z, z, (z + k) % n_z).wait_send()
        gather_copy(k, z, (z + k) % n_z).wait_send()


def fused(acts, cotangent, depth_kernel, point_weight, gain, bias):
    n_sp, n_grp, n_core = lax.axis_size("sp"), lax.axis_size("grp"), 2
    n_samples, _, cols, channels = acts.shape
    n_rows = cotangent.shape[1]
    n_parts = n_grp // n_core
    width = channels // n_sp
    part_rows = -(-width // (n_core * n_parts * 8)) * 8
    bf16, f32 = jnp.bfloat16, jnp.float32
    vmem, dma = pltpu.VMEM, pltpu.SemaphoreType.DMA
    in_vmem, anywhere = pl.BlockSpec(memory_space=pltpu.VMEM), pl.BlockSpec(memory_space=pl.ANY)
    rows = n_samples * cols
    out = pl.pallas_call(
        functools.partial(kernel, n_sp, n_grp, n_core, n_parts, part_rows),
        out_shape=(
            jax.ShapeDtypeStruct(cotangent.shape, bf16),
            jax.ShapeDtypeStruct(acts.shape, bf16),
            jax.ShapeDtypeStruct((width, channels), f32),
        ),
        in_specs=[anywhere, anywhere, in_vmem, anywhere, in_vmem, in_vmem],
        out_specs=(in_vmem, in_vmem, in_vmem),
        scratch_shapes=[
            vmem((n_rows, n_samples, cols, channels), bf16),
            vmem((n_samples, n_rows, cols, channels), bf16),
            vmem((channels, channels), bf16),
            vmem((n_rows * rows, channels), bf16),
            vmem((n_rows, rows, channels), f32),
            vmem((n_rows + 2, rows, channels), bf16),
            vmem((n_core * n_parts * part_rows, n_rows * rows), bf16),
            vmem((3, rows, channels), f32),
            vmem((n_parts, part_rows, channels), bf16),
            vmem((n_parts, part_rows, channels), bf16),
            vmem((n_parts, part_rows, channels), f32),
            vmem((n_parts, part_rows, channels), bf16),
            vmem((n_parts, part_rows, channels), bf16),
            vmem((n_core, n_parts, part_rows, channels), bf16),
            dma((3,)),
            pltpu.SemaphoreType.REGULAR((n_parts - 2, 2)),
            dma((6,)), dma((n_sp, 2)), dma((6,)), dma((n_sp, 2)),
            dma((n_parts,)), dma((n_parts,)), dma((n_parts,)), dma((n_parts,)),
            dma((n_parts,)), dma((n_parts,)), dma((n_parts,)), dma((n_parts,)),
        ],
        compiler_params=pltpu.CompilerParams(collective_id=0, has_side_effects=True),
        name="middle_flow",
    )(acts, cotangent, depth_kernel, point_weight, gain, bias)
    return out[0], out[1], out[2].reshape(-1)


def depth_forward(field, filter_weight):
    rows = field.shape[1]
    cols = field.shape[2]
    padded = jnp.pad(field, ((0, 0), (1, 1), (1, 1), (0, 0)))
    total = jnp.zeros(field.shape, jnp.float32)
    for i in range(3):
        for j in range(3):
            total = total + padded[:, i : i + rows, j : j + cols, :] * filter_weight[i, j]
    return total


def depth_backward(field, filter_weight):
    rows = field.shape[1]
    cols = field.shape[2]
    padded = jnp.pad(field, ((0, 0), (1, 1), (1, 1), (0, 0)))
    total = jnp.zeros(field.shape, jnp.float32)
    for i in range(3):
        for j in range(3):
            total = (
                total
                + padded[:, 2 - i : 2 - i + rows, 2 - j : 2 - j + cols, :] * filter_weight[i, j]
            )
    return total


def body(acts, cotangent, depth_kernel, point_weight, batch_norm_gain, norm_shift_bias):
    channel_count = acts.shape[-1]
    sample_image = lax.all_to_all(acts, "sp", split_axis=0, concat_axis=1, tiled=True)
    input_single_precision = sample_image.astype(jnp.float32)
    hidden = jnp.maximum(input_single_precision, 0.0)
    depthed = depth_forward(hidden, depth_kernel).astype(jnp.bfloat16)
    flat_d = depthed.reshape(-1, channel_count)
    element_count = flat_d.shape[0] * lax.axis_size("sp")
    projected_output = jnp.dot(flat_d, point_weight, preferred_element_type=jnp.float32)
    total, squares = lax.psum(
        (jnp.sum(projected_output, axis=0), jnp.sum(projected_output * projected_output, axis=0)),
        "sp",
    )
    batch_mean = total / element_count
    var = squares / element_count - batch_mean * batch_mean
    inverse_deviation = lax.rsqrt(var + 1e-05)
    normalized_input = (projected_output - batch_mean) * inverse_deviation
    block_out = (
        (
            input_single_precision.reshape(-1, channel_count)
            + batch_norm_gain * normalized_input
            + norm_shift_bias
        )
        .astype(jnp.bfloat16)
        .reshape(sample_image.shape)
    )
    gfloat = cotangent.astype(jnp.float32).reshape(-1, channel_count)
    scaled_output = gfloat * batch_norm_gain
    leading_layer, second_layer = lax.psum(
        (jnp.sum(scaled_output, axis=0), jnp.sum(scaled_output * normalized_input, axis=0)), "sp"
    )
    projected_gradient = (
        inverse_deviation
        * (
            scaled_output
            - leading_layer / element_count
            - normalized_input * (second_layer / element_count)
        )
    ).astype(jnp.bfloat16)
    local_weight = jnp.dot(
        flat_d.T, projected_gradient, preferred_element_type=jnp.float32
    ).reshape(-1)
    ddepth = jnp.dot(
        projected_gradient, point_weight.T, preferred_element_type=jnp.float32
    ).reshape(sample_image.shape)
    dhidden = depth_backward(ddepth, depth_kernel)
    dinput = (
        gfloat.reshape(sample_image.shape) + jnp.where(sample_image > 0, dhidden, 0.0)
    ).astype(jnp.bfloat16)
    input_grad = lax.all_to_all(dinput, "sp", split_axis=1, concat_axis=0, tiled=True)
    slices = lax.psum_scatter(
        local_weight.astype(jnp.bfloat16), "sp", scatter_dimension=0, tiled=True
    ).astype(jnp.float32)
    weight_grad = lax.psum(slices, "grp")
    return (block_out, input_grad, weight_grad)


def one_kernel_fits(mesh, acts, cotangent):
    n_sp, n_grp = mesh.shape["sp"], mesh.shape["grp"]
    group_elements = acts.size // n_grp
    return (
        acts.shape[1] == n_sp
        and acts.shape[0] == n_sp * n_grp
        and acts.shape[2] % 16 == 0
        and acts.shape[3] % n_sp == 0
        and n_grp % 4 == 0
        and n_sp == 4
        and group_elements <= 1 << 20
    )


def solution(mesh):
    in_specs = (P("grp", "sp", None, None), P(("grp", "sp"), None, None, None), P(), P(), P(), P())
    out_specs = (P(("grp", "sp"), None, None, None), P("grp", "sp", None, None), P("sp"))

    def step(acts, cotangent, *params):
        inner = fused if one_kernel_fits(mesh, acts, cotangent) else body
        mapped = jax.shard_map(
            inner, mesh=mesh, in_specs=in_specs, out_specs=out_specs, check_vma=False
        )
        return mapped(acts, cotangent, *params)

    return step
```

```python
import functools
import math

import jax
import jax.numpy as jnp
from jax import lax
from jax.experimental import pallas as pl
from jax.experimental.pallas import tpu as pltpu
from jax.sharding import PartitionSpec as P

MESH = pl.DeviceIdType.MESH
LANES = 128
NT = (((1,), (1,)), ((), ()))


def lane_blocks(channels):
    return [slice(at, min(at + LANES, channels)) for at in range(0, channels, LANES)]


def column_shift(field, step):
    cols = field.shape[0]
    at = lax.broadcasted_iota(jnp.int32, field.shape, 0)
    keep = (at >= 1) if step > 0 else (at < cols - 1)
    return jnp.where(keep, pltpu.roll(field, step % cols, 0), 0.0)


def kernel(
    n_sp, n_grp, n_core, n_parts, part_rows,
    acts_ref, cot_ref, dk_ref, pw_hbm, gain_ref, bias_ref,
    block_out_ref, input_grad_ref, weight_ref,
    ga, gc, pw, d_ref, p_ref, dp_ref, dsel_ref, dd_ref,
    pair_send, pair_recv, own_ref, z_send, z_recv, res_ref, flat_rows,
    local_sem, ready, a_send, a_recv, c_send, c_recv,
    pair_ssem, pair_rsem, z_ssem, z_rsem, g_ssem, g_rsem, f_ssem, f_rsem,
):
    sp = lax.axis_index("sp")
    grp = lax.axis_index("grp")
    n_z = n_grp // n_core
    z, core = grp // n_core, grp % n_core
    other = (core + 1) % n_core
    partner = z * n_core + other
    middle = n_z // 2
    toward = z + 1 - 2 * (z // middle)
    away = 2 * z - toward
    inner = (z > 0) & (z < n_z - 1)
    side = int(n_sp**0.5)
    sx = (sp // side) * side + (sp + 1) % side
    sy = (sp + side) % n_sp
    far = (sx + side) % n_sp
    n_rows, n_samples, cols, channels = ga.shape
    count = n_rows * n_samples * cols
    blocks = lane_blocks(channels)

    load_pw = pltpu.make_async_copy(pw_hbm, pw, local_sem.at[0])
    load_pw.start()
    own_acts = pltpu.make_async_copy(acts_ref.at[:, 0], ga.at[sp], local_sem.at[1])
    own_acts.start()
    own_cot = pltpu.make_async_copy(cot_ref.at[0], gc.at[sp], local_sem.at[2])
    own_cot.start()

    barrier = pltpu.get_barrier_semaphore()

    def greet(peer):
        pl.semaphore_signal(barrier, inc=1, device_id=peer, device_id_type=MESH)

    def z_core(at):
        return {"grp": at * n_core + core}

    peers = [{"sp": sx}, {"sp": sy}, {"grp": partner}, z_core(toward)]
    for peer in peers:
        greet(peer)

    @pl.when(inner)
    def _():
        greet(z_core(away))
        pl.semaphore_wait(barrier, len(peers) + 1)

    @pl.when(jnp.logical_not(inner))
    def _():
        pl.semaphore_wait(barrier, len(peers))

    class Gather:
        def __init__(self, own, buf, send, recv):
            self.own, self.buf, self.send, self.recv = own, buf, send, recv
            self.size = buf.shape[1] // 2

        def part(self, half):
            return pl.ds(half * self.size, self.size)

        def copy(self, k, src, slot, half, to):
            return pltpu.make_async_remote_copy(
                src_ref=src, dst_ref=self.buf.at[slot, self.part(half)],
                send_sem=self.send.at[k], recv_sem=self.recv.at[slot, half],
                device_id={"sp": to}, device_id_type=MESH,
            )

        def direct(self):
            return [
                self.copy(k, self.own.at[self.part(half)], sp, half, to)
                for k, (half, to) in enumerate(((0, sx), (1, sy), (1, sx), (0, sy)))
            ]

        def start_relayed(self):
            for copy in self.direct()[:2]:
                copy.start()

        def start_rest(self):
            for copy in self.direct()[2:]:
                copy.start()

        def relays(self):
            return [
                self.copy(4, self.buf.at[sx, self.part(0)], sx, 0, sy),
                self.copy(5, self.buf.at[sy, self.part(1)], sy, 1, sx),
            ]

        def arrived(self, slot, half):
            self.copy(0, self.buf.at[slot, self.part(half)], slot, half, sx).wait_recv()

        def relay(self):
            for copy, slot, half in zip(self.relays(), (sx, sy), (0, 1)):
                self.arrived(slot, half)
                copy.start()

        def finish(self):
            for slot, half in ((sx, 1), (sy, 0), (far, 0), (far, 1)):
                self.arrived(slot, half)

        def sent(self):
            for copy in self.direct() + self.relays():
                copy.wait_send()

    acts_gather = Gather(acts_ref.at[:, 0], ga, a_send, a_recv)
    cot_gather = Gather(cot_ref.at[0], gc, c_send, c_recv)
    acts_gather.start_relayed()
    acts_gather.start_rest()
    cot_gather.start_relayed()
    flat_rows[...] = jnp.zeros(flat_rows.shape, flat_rows.dtype)
    dp_ref[0] = jnp.zeros(dp_ref.shape[1:], dp_ref.dtype)
    dp_ref[n_rows + 1] = jnp.zeros(dp_ref.shape[1:], dp_ref.dtype)
    acts_gather.relay()
    cot_gather.start_rest()
    for level in range(n_z - 2):
        for step in (1, -1):
            there = (z + step >= 0) & (z + step < n_z)

            @pl.when(there)
            def _():
                pl.semaphore_signal(
                    ready.at[level, (1 - step) // 2], inc=1,
                    device_id=z_core(z + step), device_id_type=MESH,
                )

        for step in (1, -1):
            there = (z + step >= 0) & (z + step < n_z)

            @pl.when(there)
            def _():
                pl.semaphore_wait(ready.at[level, (1 + step) // 2], 1)

    own_acts.wait()
    load_pw.wait()
    cot_gather.relay()
    acts_gather.finish()

    @pl.loop(0, n_samples)
    def _(b):
        for lanes in blocks:
            h = [jnp.maximum(ga[r, b, :, lanes].astype(jnp.float32), 0.0) for r in range(n_rows)]
            taps = [[dk_ref[i, j : j + 1, lanes] for j in range(3)] for i in range(3)]
            for r in range(n_rows):
                t = [
                    sum(h[r + i - 1] * taps[i][j] for i in range(3) if 0 <= r + i - 1 < n_rows)
                    for j in range(3)
                ]
                total = t[1] + column_shift(t[0], 1) + column_shift(t[2], -1)
                at = pl.multiple_of((r * n_samples + b) * cols, cols)
                d_ref[pl.ds(at, cols), lanes] = total.astype(jnp.bfloat16)

    p_ref[...] = jnp.dot(
        d_ref[...], pw[...], preferred_element_type=jnp.float32
    ).reshape(p_ref.shape)
    sel_rows = dsel_ref.shape[0]
    width = channels // n_sp
    row = lax.broadcasted_iota(jnp.int32, (sel_rows, channels), 0)
    lane = lax.broadcasted_iota(jnp.int32, (sel_rows, channels), 1)
    pick = jnp.where((lane - sp * width == row) & (row < width), 1.0, 0.0).astype(jnp.bfloat16)
    dsel_ref[...] = lax.dot_general(
        pick, d_ref[...], NT, preferred_element_type=jnp.float32
    ).astype(jnp.bfloat16)

    own_cot.wait()
    cot_gather.finish()

    means, rstds = [], []
    for lanes in blocks:
        size = lanes.stop - lanes.start
        s1 = s2 = sg = sgp = jnp.zeros((cols, size), jnp.float32)
        for r in range(n_rows):
            for b in range(n_samples):
                p = p_ref[r, b * cols : (b + 1) * cols, lanes]
                g = gc[b, r, :, lanes].astype(jnp.float32)
                s1, s2, sg, sgp = s1 + p, s2 + p * p, sg + g, sgp + g * p
        s1, s2, sg, sgp = [jnp.sum(s, axis=0, keepdims=True) for s in (s1, s2, sg, sgp)]
        gain = gain_ref[lanes].reshape(1, -1)
        mean = s1 / count
        var = s2 / count - mean * mean
        rstd = lax.rsqrt(var + 1e-05)
        a1 = gain * sg / count
        a2 = gain * rstd * (sgp - mean * sg) / count
        means.append(mean)
        rstds.append(rstd)
        for r in range(n_rows):
            for b in range(n_samples):
                p = p_ref[r, b * cols : (b + 1) * cols, lanes]
                g = gc[b, r, :, lanes].astype(jnp.float32)
                xhat = (p - mean) * rstd
                dp_ref[r + 1, b * cols : (b + 1) * cols, lanes] = (
                    rstd * (g * gain - a1 - xhat * a2)
                ).astype(jnp.bfloat16)

    half = n_parts * part_rows

    def product(which):
        left = dsel_ref[pl.ds(pl.multiple_of(which * half, half), half), :]
        return jnp.dot(
            left, dp_ref[1 : n_rows + 1].reshape(-1, channels), preferred_element_type=jnp.float32
        ).reshape(n_parts, part_rows, channels)

    def pair_copy(k):
        return pltpu.make_async_remote_copy(
            src_ref=pair_send.at[k], dst_ref=pair_recv.at[k],
            send_sem=pair_ssem.at[k], recv_sem=pair_rsem.at[k],
            device_id={"grp": partner}, device_id_type=MESH,
        )

    def z_copy(k, slot, to):
        return pltpu.make_async_remote_copy(
            src_ref=z_send.at[k], dst_ref=z_recv.at[slot],
            send_sem=z_ssem.at[k], recv_sem=z_rsem.at[slot],
            device_id=z_core(to), device_id_type=MESH,
        )

    def gather_copy(k, slot, to):
        return pltpu.make_async_remote_copy(
            src_ref=res_ref.at[core, slot], dst_ref=res_ref.at[core, slot],
            send_sem=g_ssem.at[k], recv_sem=g_rsem.at[slot],
            device_id=z_core(to), device_id_type=MESH,
        )

    def forward_copy(k, owner):
        return pltpu.make_async_remote_copy(
            src_ref=res_ref.at[owner, k], dst_ref=res_ref.at[owner, k],
            send_sem=f_ssem.at[k], recv_sem=f_rsem.at[k],
            device_id={"grp": partner}, device_id_type=MESH,
        )

    def outputs(at):
        lanes = blocks[at]
        taps = [[dk_ref[i, j : j + 1, lanes] for j in range(3)] for i in range(3)]
        gain, bias = gain_ref[lanes].reshape(1, -1), bias_ref[lanes].reshape(1, -1)
        for b in range(n_samples):
            own = slice(b * cols, (b + 1) * cols)
            dd = [dd_ref[i, own, lanes] for i in range(3)]
            t = [sum(dd[2 - i] * taps[i][j] for i in range(3)) for j in range(3)]
            dh = t[1] + column_shift(t[0], -1) + column_shift(t[2], 1)
            a = ga[sp, b, :, lanes].astype(jnp.float32)
            g = gc[b, sp, :, lanes].astype(jnp.float32)
            input_grad_ref[b, 0, :, lanes] = (g + jnp.where(a > 0, dh, 0.0)).astype(jnp.bfloat16)
        for r in range(n_rows):
            p = p_ref[r, pl.ds(pl.multiple_of(sp * cols, cols), cols), lanes]
            a = ga[r, sp, :, lanes].astype(jnp.float32)
            block_out_ref[0, r, :, lanes] = (
                a + gain * ((p - means[at]) * rstds[at]) + bias
            ).astype(jnp.bfloat16)

    def write(owner, k):
        at = (owner * n_parts + k) * part_rows
        for c, lanes in enumerate(blocks):
            size = lanes.stop - lanes.start
            flat_rows[c, at : at + part_rows, :size] = res_ref[owner, k, :, lanes].astype(
                jnp.float32
            )

    def flatten():
        period = LANES // math.gcd(channels, LANES)
        step = channels * period // LANES
        runs = flat_rows.shape[1] // period
        at = lax.broadcasted_iota(jnp.int32, (runs, LANES), 1)
        last = None
        for r in range(period):
            row, shift = divmod(channels * r, LANES)
            parts = [flat_rows[c, pl.ds(r, runs, stride=period), :] for c in range(len(blocks))]
            if shift:
                parts = [pltpu.roll(part, shift, 1) for part in parts]
                zero = jnp.zeros((runs, LANES), jnp.float32)
                parts = [
                    jnp.where(at < shift, before, part)
                    for before, part in zip([zero] + parts, parts + [zero])
                ]
                parts[0] = parts[0] + last
            used = -(-(shift + channels) // LANES)
            ends = (shift + channels) % LANES == 0
            for c in range(used if ends else used - 1):
                weight_ref[pl.ds(row + c, runs, stride=step), :] = parts[c]
            last = parts[used - 1]

    pair_send[...] = product(other).astype(jnp.bfloat16)
    for k in range(1, n_z + 1):
        pair_copy((z + k) % n_z).start()
    own_ref[...] = product(core)
    for k in range(1, n_z):
        to = (z + k) % n_z
        pair_copy(to).wait_recv()
        z_send[to] = (own_ref[to] + pair_recv[to].astype(jnp.float32)).astype(jnp.bfloat16)
        z_copy(to, z, to).start()

    dd_ref[...] = lax.dot_general(
        dp_ref[pl.ds(sp, 3)].reshape(-1, channels), pw[...], NT,
        preferred_element_type=jnp.float32,
    ).reshape(dd_ref.shape)

    pair_copy(z).wait_recv()
    mine = own_ref[z] + pair_recv[z].astype(jnp.float32)
    for k in range(1, n_z):
        slot = (z + k) % n_z
        z_copy(slot, slot, z).wait_recv()
        mine = mine + z_recv[slot].astype(jnp.float32)
    res_ref[core, z] = mine.astype(jnp.bfloat16)
    for k in range(1, n_z):
        gather_copy(k, z, (z + k) % n_z).start()
    forward_copy(z, core).start()

    for at in range(len(blocks)):
        outputs(at)

    for k in range(1, n_z):
        slot = (z + k) % n_z
        gather_copy(k, slot, z).wait_recv()
        forward_copy(slot, core).start()
    for k in range(n_z):
        forward_copy((z + k) % n_z, other).wait_recv()
    for owner in range(n_core):
        for k in range(n_z):
            write(owner, k)
    flatten()

    acts_gather.sent()
    cot_gather.sent()
    for k in range(n_z):
        pair_copy(k).wait_send()
        forward_copy(k, core).wait_send()
    for k in range(1, n_z):
        z_copy((z + k) % n_z, z, (z + k) % n_z).wait_send()
        gather_copy(k, z, (z + k) % n_z).wait_send()


def fused(acts, cotangent, depth_kernel, point_weight, gain, bias):
    n_sp, n_grp, n_core = lax.axis_size("sp"), lax.axis_size("grp"), 2
    n_samples, _, cols, channels = acts.shape
    n_rows = cotangent.shape[1]
    n_parts = n_grp // n_core
    width = channels // n_sp
    part_rows = -(-width // (n_core * n_parts * 8)) * 8
    period = LANES // math.gcd(channels, LANES)
    padded = -(-n_core * n_parts * part_rows // period) * period
    bf16, f32 = jnp.bfloat16, jnp.float32
    vmem, dma = pltpu.VMEM, pltpu.SemaphoreType.DMA
    in_vmem, anywhere = pl.BlockSpec(memory_space=pltpu.VMEM), pl.BlockSpec(memory_space=pl.ANY)
    rows = n_samples * cols
    out = pl.pallas_call(
        functools.partial(kernel, n_sp, n_grp, n_core, n_parts, part_rows),
        out_shape=(
            jax.ShapeDtypeStruct(cotangent.shape, bf16),
            jax.ShapeDtypeStruct(acts.shape, bf16),
            jax.ShapeDtypeStruct((padded * channels // LANES, LANES), f32),
        ),
        in_specs=[anywhere, anywhere, in_vmem, anywhere, in_vmem, in_vmem],
        out_specs=(in_vmem, in_vmem, in_vmem),
        scratch_shapes=[
            vmem((n_rows, n_samples, cols, channels), bf16),
            vmem((n_samples, n_rows, cols, channels), bf16),
            vmem((channels, channels), bf16),
            vmem((n_rows * rows, channels), bf16),
            vmem((n_rows, rows, channels), f32),
            vmem((n_rows + 2, rows, channels), bf16),
            vmem((n_core * n_parts * part_rows, n_rows * rows), bf16),
            vmem((3, rows, channels), f32),
            vmem((n_parts, part_rows, channels), bf16),
            vmem((n_parts, part_rows, channels), bf16),
            vmem((n_parts, part_rows, channels), f32),
            vmem((n_parts, part_rows, channels), bf16),
            vmem((n_parts, part_rows, channels), bf16),
            vmem((n_core, n_parts, part_rows, channels), bf16),
            vmem((len(lane_blocks(channels)), padded, LANES), f32),
            dma((3,)),
            pltpu.SemaphoreType.REGULAR((n_parts - 2, 2)),
            dma((6,)), dma((n_sp, 2)), dma((6,)), dma((n_sp, 2)),
            dma((n_parts,)), dma((n_parts,)), dma((n_parts,)), dma((n_parts,)),
            dma((n_parts,)), dma((n_parts,)), dma((n_parts,)), dma((n_parts,)),
        ],
        compiler_params=pltpu.CompilerParams(collective_id=0, has_side_effects=True),
        name="middle_flow",
    )(acts, cotangent, depth_kernel, point_weight, gain, bias)
    return out[0], out[1], out[2].reshape(-1)[: width * channels]


def depth_forward(field, filter_weight):
    rows = field.shape[1]
    cols = field.shape[2]
    padded = jnp.pad(field, ((0, 0), (1, 1), (1, 1), (0, 0)))
    total = jnp.zeros(field.shape, jnp.float32)
    for i in range(3):
        for j in range(3):
            total = total + padded[:, i : i + rows, j : j + cols, :] * filter_weight[i, j]
    return total


def depth_backward(field, filter_weight):
    rows = field.shape[1]
    cols = field.shape[2]
    padded = jnp.pad(field, ((0, 0), (1, 1), (1, 1), (0, 0)))
    total = jnp.zeros(field.shape, jnp.float32)
    for i in range(3):
        for j in range(3):
            total = (
                total
                + padded[:, 2 - i : 2 - i + rows, 2 - j : 2 - j + cols, :] * filter_weight[i, j]
            )
    return total


def body(acts, cotangent, depth_kernel, point_weight, batch_norm_gain, norm_shift_bias):
    channel_count = acts.shape[-1]
    sample_image = lax.all_to_all(acts, "sp", split_axis=0, concat_axis=1, tiled=True)
    input_single_precision = sample_image.astype(jnp.float32)
    hidden = jnp.maximum(input_single_precision, 0.0)
    depthed = depth_forward(hidden, depth_kernel).astype(jnp.bfloat16)
    flat_d = depthed.reshape(-1, channel_count)
    element_count = flat_d.shape[0] * lax.axis_size("sp")
    projected_output = jnp.dot(flat_d, point_weight, preferred_element_type=jnp.float32)
    total, squares = lax.psum(
        (jnp.sum(projected_output, axis=0), jnp.sum(projected_output * projected_output, axis=0)),
        "sp",
    )
    batch_mean = total / element_count
    var = squares / element_count - batch_mean * batch_mean
    inverse_deviation = lax.rsqrt(var + 1e-05)
    normalized_input = (projected_output - batch_mean) * inverse_deviation
    block_out = (
        (
            input_single_precision.reshape(-1, channel_count)
            + batch_norm_gain * normalized_input
            + norm_shift_bias
        )
        .astype(jnp.bfloat16)
        .reshape(sample_image.shape)
    )
    gfloat = cotangent.astype(jnp.float32).reshape(-1, channel_count)
    scaled_output = gfloat * batch_norm_gain
    leading_layer, second_layer = lax.psum(
        (jnp.sum(scaled_output, axis=0), jnp.sum(scaled_output * normalized_input, axis=0)), "sp"
    )
    projected_gradient = (
        inverse_deviation
        * (
            scaled_output
            - leading_layer / element_count
            - normalized_input * (second_layer / element_count)
        )
    ).astype(jnp.bfloat16)
    local_weight = jnp.dot(
        flat_d.T, projected_gradient, preferred_element_type=jnp.float32
    ).reshape(-1)
    ddepth = jnp.dot(
        projected_gradient, point_weight.T, preferred_element_type=jnp.float32
    ).reshape(sample_image.shape)
    dhidden = depth_backward(ddepth, depth_kernel)
    dinput = (
        gfloat.reshape(sample_image.shape) + jnp.where(sample_image > 0, dhidden, 0.0)
    ).astype(jnp.bfloat16)
    input_grad = lax.all_to_all(dinput, "sp", split_axis=1, concat_axis=0, tiled=True)
    slices = lax.psum_scatter(
        local_weight.astype(jnp.bfloat16), "sp", scatter_dimension=0, tiled=True
    ).astype(jnp.float32)
    weight_grad = lax.psum(slices, "grp")
    return (block_out, input_grad, weight_grad)


def one_kernel_fits(mesh, acts, cotangent):
    n_sp, n_grp = mesh.shape["sp"], mesh.shape["grp"]
    group_elements = acts.size // n_grp
    return (
        acts.shape[1] == n_sp
        and acts.shape[0] == n_sp * n_grp
        and acts.shape[2] % 16 == 0
        and acts.shape[3] % n_sp == 0
        and n_grp % 4 == 0
        and n_sp == 4
        and group_elements <= 1 << 20
    )


def solution(mesh):
    in_specs = (P("grp", "sp", None, None), P(("grp", "sp"), None, None, None), P(), P(), P(), P())
    out_specs = (P(("grp", "sp"), None, None, None), P("grp", "sp", None, None), P("sp"))

    def step(acts, cotangent, *params):
        inner = fused if one_kernel_fits(mesh, acts, cotangent) else body
        mapped = jax.shard_map(
            inner, mesh=mesh, in_specs=in_specs, out_specs=out_specs, check_vma=False
        )
        return mapped(acts, cotangent, *params)

    return step
```

```python
import functools
import math

import jax
import jax.numpy as jnp
from jax import lax
from jax.experimental import pallas as pl
from jax.experimental.pallas import tpu as pltpu
from jax.sharding import PartitionSpec as P

MESH = pl.DeviceIdType.MESH
LANES = 128
NT = (((1,), (1,)), ((), ()))


def lane_blocks(channels):
    return [slice(at, min(at + LANES, channels)) for at in range(0, channels, LANES)]


def column_shift(field, step):
    cols = field.shape[0]
    at = lax.broadcasted_iota(jnp.int32, field.shape, 0)
    keep = (at >= 1) if step > 0 else (at < cols - 1)
    return jnp.where(keep, pltpu.roll(field, step % cols, 0), 0.0)


def kernel(
    n_sp, n_grp, n_core, n_parts, part_rows,
    acts_ref, cot_ref, dk_ref, pw_hbm, gain_ref, bias_ref,
    block_out_ref, input_grad_ref, weight_ref,
    ga, gc, pw, d_ref, p_ref, dp_ref, dsel_ref, dd_ref,
    pair_send, pair_recv, own_ref, z_send, z_recv, res_ref, flat_rows,
    local_sem, ready, a_send, a_recv, c_send, c_recv,
    pair_ssem, pair_rsem, z_ssem, z_rsem, g_ssem, g_rsem, f_ssem, f_rsem,
):
    sp = lax.axis_index("sp")
    grp = lax.axis_index("grp")
    n_z = n_grp // n_core
    z, core = grp // n_core, grp % n_core
    other = (core + 1) % n_core
    partner = z * n_core + other
    middle = n_z // 2
    toward = z + 1 - 2 * (z // middle)
    away = 2 * z - toward
    inner = (z > 0) & (z < n_z - 1)
    side = int(n_sp**0.5)
    sx = (sp // side) * side + (sp + 1) % side
    sy = (sp + side) % n_sp
    far = (sx + side) % n_sp
    n_rows, n_samples, cols, channels = ga.shape
    count = n_rows * n_samples * cols
    blocks = lane_blocks(channels)

    load_pw = pltpu.make_async_copy(pw_hbm, pw, local_sem.at[0])
    load_pw.start()
    own_acts = pltpu.make_async_copy(acts_ref.at[:, 0], ga.at[sp], local_sem.at[1])
    own_acts.start()
    own_cot = pltpu.make_async_copy(cot_ref.at[0], gc.at[sp], local_sem.at[2])
    own_cot.start()

    barrier = pltpu.get_barrier_semaphore()

    def greet(peer):
        pl.semaphore_signal(barrier, inc=1, device_id=peer, device_id_type=MESH)

    def z_core(at):
        return {"grp": at * n_core + core}

    peers = [{"sp": sx}, {"sp": sy}, {"grp": partner}, z_core(toward)]
    for peer in peers:
        greet(peer)

    @pl.when(inner)
    def _():
        greet(z_core(away))
        pl.semaphore_wait(barrier, len(peers) + 1)

    @pl.when(jnp.logical_not(inner))
    def _():
        pl.semaphore_wait(barrier, len(peers))

    class Gather:
        def __init__(self, own, buf, send, recv):
            self.own, self.buf, self.send, self.recv = own, buf, send, recv
            self.size = buf.shape[1] // 2

        def part(self, half):
            return pl.ds(half * self.size, self.size)

        def copy(self, k, src, slot, half, to):
            return pltpu.make_async_remote_copy(
                src_ref=src, dst_ref=self.buf.at[slot, self.part(half)],
                send_sem=self.send.at[k], recv_sem=self.recv.at[slot, half],
                device_id={"sp": to}, device_id_type=MESH,
            )

        def direct(self):
            return [
                self.copy(k, self.own.at[self.part(half)], sp, half, to)
                for k, (half, to) in enumerate(((0, sx), (1, sy), (1, sx), (0, sy)))
            ]

        def start_relayed(self):
            for copy in self.direct()[:2]:
                copy.start()

        def start_rest(self):
            for copy in self.direct()[2:]:
                copy.start()

        def relays(self):
            return [
                self.copy(4, self.buf.at[sx, self.part(0)], sx, 0, sy),
                self.copy(5, self.buf.at[sy, self.part(1)], sy, 1, sx),
            ]

        def arrived(self, slot, half):
            self.copy(0, self.buf.at[slot, self.part(half)], slot, half, sx).wait_recv()

        def relay(self):
            for copy, slot, half in zip(self.relays(), (sx, sy), (0, 1)):
                self.arrived(slot, half)
                copy.start()

        def finish(self):
            for slot, half in ((sx, 1), (sy, 0), (far, 0), (far, 1)):
                self.arrived(slot, half)

        def sent(self):
            for copy in self.direct() + self.relays():
                copy.wait_send()

    acts_gather = Gather(acts_ref.at[:, 0], ga, a_send, a_recv)
    cot_gather = Gather(cot_ref.at[0], gc, c_send, c_recv)
    acts_gather.start_relayed()
    acts_gather.start_rest()
    cot_gather.start_relayed()
    flat_rows[...] = jnp.zeros(flat_rows.shape, flat_rows.dtype)
    dp_ref[0] = jnp.zeros(dp_ref.shape[1:], dp_ref.dtype)
    dp_ref[n_rows + 1] = jnp.zeros(dp_ref.shape[1:], dp_ref.dtype)
    acts_gather.relay()
    cot_gather.start_rest()
    for level in range(n_z - 2):
        for step in (1, -1):
            there = (z + step >= 0) & (z + step < n_z)

            @pl.when(there)
            def _():
                pl.semaphore_signal(
                    ready.at[level, (1 - step) // 2], inc=1,
                    device_id=z_core(z + step), device_id_type=MESH,
                )

        for step in (1, -1):
            there = (z + step >= 0) & (z + step < n_z)

            @pl.when(there)
            def _():
                pl.semaphore_wait(ready.at[level, (1 + step) // 2], 1)

    own_acts.wait()
    load_pw.wait()
    cot_gather.relay()
    acts_gather.finish()

    @pl.loop(0, n_samples)
    def _(b):
        for lanes in blocks:
            h = [jnp.maximum(ga[r, b, :, lanes].astype(jnp.float32), 0.0) for r in range(n_rows)]
            taps = [[dk_ref[i, j : j + 1, lanes] for j in range(3)] for i in range(3)]
            for r in range(n_rows):
                t = [
                    sum(h[r + i - 1] * taps[i][j] for i in range(3) if 0 <= r + i - 1 < n_rows)
                    for j in range(3)
                ]
                total = t[1] + column_shift(t[0], 1) + column_shift(t[2], -1)
                at = pl.multiple_of((r * n_samples + b) * cols, cols)
                d_ref[pl.ds(at, cols), lanes] = total.astype(jnp.bfloat16)

    p_ref[...] = jnp.dot(
        d_ref[...], pw[...], preferred_element_type=jnp.float32
    ).reshape(p_ref.shape)
    sel_rows = dsel_ref.shape[0]
    width = channels // n_sp
    row = lax.broadcasted_iota(jnp.int32, (sel_rows, channels), 0)
    lane = lax.broadcasted_iota(jnp.int32, (sel_rows, channels), 1)
    pick = jnp.where((lane - sp * width == row) & (row < width), 1.0, 0.0).astype(jnp.bfloat16)
    dsel_ref[...] = lax.dot_general(
        pick, d_ref[...], NT, preferred_element_type=jnp.float32
    ).astype(jnp.bfloat16)

    own_cot.wait()
    cot_gather.finish()

    means, rstds = [], []
    for lanes in blocks:
        size = lanes.stop - lanes.start
        s1 = s2 = sg = sgp = jnp.zeros((cols, size), jnp.float32)
        for r in range(n_rows):
            for b in range(n_samples):
                p = p_ref[r, b * cols : (b + 1) * cols, lanes]
                g = gc[b, r, :, lanes].astype(jnp.float32)
                s1, s2, sg, sgp = s1 + p, s2 + p * p, sg + g, sgp + g * p
        s1, s2, sg, sgp = [jnp.sum(s, axis=0, keepdims=True) for s in (s1, s2, sg, sgp)]
        gain = gain_ref[lanes].reshape(1, -1)
        mean = s1 / count
        var = s2 / count - mean * mean
        rstd = lax.rsqrt(var + 1e-05)
        a1 = gain * sg / count
        a2 = gain * rstd * (sgp - mean * sg) / count
        means.append(mean)
        rstds.append(rstd)
        for r in range(n_rows):
            for b in range(n_samples):
                p = p_ref[r, b * cols : (b + 1) * cols, lanes]
                g = gc[b, r, :, lanes].astype(jnp.float32)
                xhat = (p - mean) * rstd
                dp_ref[r + 1, b * cols : (b + 1) * cols, lanes] = (
                    rstd * (g * gain - a1 - xhat * a2)
                ).astype(jnp.bfloat16)

    half = n_parts * part_rows

    def product(which):
        left = dsel_ref[pl.ds(pl.multiple_of(which * half, half), half), :]
        return jnp.dot(
            left, dp_ref[1 : n_rows + 1].reshape(-1, channels), preferred_element_type=jnp.float32
        ).reshape(n_parts, part_rows, channels)

    def pair_copy(k):
        return pltpu.make_async_remote_copy(
            src_ref=pair_send.at[k], dst_ref=pair_recv.at[k],
            send_sem=pair_ssem.at[k], recv_sem=pair_rsem.at[k],
            device_id={"grp": partner}, device_id_type=MESH,
        )

    def z_copy(k, slot, to):
        return pltpu.make_async_remote_copy(
            src_ref=z_send.at[k], dst_ref=z_recv.at[slot],
            send_sem=z_ssem.at[k], recv_sem=z_rsem.at[slot],
            device_id=z_core(to), device_id_type=MESH,
        )

    def gather_copy(k, slot, to):
        return pltpu.make_async_remote_copy(
            src_ref=res_ref.at[core, slot], dst_ref=res_ref.at[core, slot],
            send_sem=g_ssem.at[k], recv_sem=g_rsem.at[slot],
            device_id=z_core(to), device_id_type=MESH,
        )

    def forward_copy(k, owner):
        return pltpu.make_async_remote_copy(
            src_ref=res_ref.at[owner, k], dst_ref=res_ref.at[owner, k],
            send_sem=f_ssem.at[k], recv_sem=f_rsem.at[k],
            device_id={"grp": partner}, device_id_type=MESH,
        )

    def outputs(at):
        lanes = blocks[at]
        taps = [[dk_ref[i, j : j + 1, lanes] for j in range(3)] for i in range(3)]
        gain, bias = gain_ref[lanes].reshape(1, -1), bias_ref[lanes].reshape(1, -1)
        for b in range(n_samples):
            own = slice(b * cols, (b + 1) * cols)
            dd = [dd_ref[i, own, lanes] for i in range(3)]
            t = [sum(dd[2 - i] * taps[i][j] for i in range(3)) for j in range(3)]
            dh = t[1] + column_shift(t[0], -1) + column_shift(t[2], 1)
            a = ga[sp, b, :, lanes].astype(jnp.float32)
            g = gc[b, sp, :, lanes].astype(jnp.float32)
            input_grad_ref[b, 0, :, lanes] = (g + jnp.where(a > 0, dh, 0.0)).astype(jnp.bfloat16)
        for r in range(n_rows):
            p = p_ref[r, pl.ds(pl.multiple_of(sp * cols, cols), cols), lanes]
            a = ga[r, sp, :, lanes].astype(jnp.float32)
            block_out_ref[0, r, :, lanes] = (
                a + gain * ((p - means[at]) * rstds[at]) + bias
            ).astype(jnp.bfloat16)

    def write(owner, k):
        at = (owner * n_parts + k) * part_rows
        for c, lanes in enumerate(blocks):
            size = lanes.stop - lanes.start
            flat_rows[c, at : at + part_rows, :size] = res_ref[owner, k, :, lanes].astype(
                jnp.float32
            )

    def flatten():
        period = LANES // math.gcd(channels, LANES)
        step = channels * period // LANES
        runs = flat_rows.shape[1] // period
        at = lax.broadcasted_iota(jnp.int32, (runs, LANES), 1)
        last = None
        for r in range(period):
            row, shift = divmod(channels * r, LANES)
            parts = [flat_rows[c, pl.ds(r, runs, stride=period), :] for c in range(len(blocks))]
            if shift:
                parts = [pltpu.roll(part, shift, 1) for part in parts]
                zero = jnp.zeros((runs, LANES), jnp.float32)
                parts = [
                    jnp.where(at < shift, before, part)
                    for before, part in zip([zero] + parts, parts + [zero])
                ]
                parts[0] = parts[0] + last
            used = -(-(shift + channels) // LANES)
            ends = (shift + channels) % LANES == 0
            for c in range(used if ends else used - 1):
                weight_ref[pl.ds(row + c, runs, stride=step), :] = parts[c]
            last = parts[used - 1]

    pair_send[...] = product(other).astype(jnp.bfloat16)
    for k in range(1, n_z + 1):
        pair_copy((z + k) % n_z).start()
    own_ref[...] = product(core)
    for k in range(1, n_z):
        to = (z + k) % n_z
        pair_copy(to).wait_recv()
        z_send[to] = (own_ref[to] + pair_recv[to].astype(jnp.float32)).astype(jnp.bfloat16)
        z_copy(to, z, to).start()

    dd_ref[...] = lax.dot_general(
        dp_ref[pl.ds(sp, 3)].reshape(-1, channels), pw[...], NT,
        preferred_element_type=jnp.float32,
    ).reshape(dd_ref.shape)

    pair_copy(z).wait_recv()
    mine = own_ref[z] + pair_recv[z].astype(jnp.float32)
    for k in range(1, n_z):
        slot = (z + k) % n_z
        z_copy(slot, slot, z).wait_recv()
        mine = mine + z_recv[slot].astype(jnp.float32)
    res_ref[core, z] = mine.astype(jnp.bfloat16)
    for k in range(1, n_z):
        gather_copy(k, z, (z + k) % n_z).start()
    forward_copy(z, core).start()

    for at in range(len(blocks)):
        outputs(at)

    for k in range(1, n_z):
        slot = (z + k) % n_z
        gather_copy(k, slot, z).wait_recv()
        forward_copy(slot, core).start()
    for k in range(n_z):
        forward_copy((z + k) % n_z, other).wait_recv()
    for owner in range(n_core):
        for k in range(n_z):
            write(owner, k)
    flatten()

    acts_gather.sent()
    cot_gather.sent()
    for k in range(n_z):
        pair_copy(k).wait_send()
        forward_copy(k, core).wait_send()
    for k in range(1, n_z):
        z_copy((z + k) % n_z, z, (z + k) % n_z).wait_send()
        gather_copy(k, z, (z + k) % n_z).wait_send()


def finish(block_ref, grad_ref, weight_ref, block_out_ref, grad_out_ref, flat_ref):
    block_out_ref[...] = block_ref[...]
    grad_out_ref[...] = grad_ref[...]
    size, tile = flat_ref.shape[0], 8 * LANES
    for at in range(0, size, tile):
        part = weight_ref[at // LANES : at // LANES + 8].reshape(tile)
        left = min(tile, size - at)
        flat_ref[at : at + left] = part[:left]


def fused(acts, cotangent, depth_kernel, point_weight, gain, bias):
    n_sp, n_grp, n_core = lax.axis_size("sp"), lax.axis_size("grp"), 2
    n_samples, _, cols, channels = acts.shape
    n_rows = cotangent.shape[1]
    n_parts = n_grp // n_core
    width = channels // n_sp
    part_rows = -(-width // (n_core * n_parts * 8)) * 8
    period = LANES // math.gcd(channels, LANES)
    padded = -(-n_core * n_parts * part_rows // period) * period
    bf16, f32 = jnp.bfloat16, jnp.float32
    vmem, dma = pltpu.VMEM, pltpu.SemaphoreType.DMA
    in_vmem, anywhere = pl.BlockSpec(memory_space=pltpu.VMEM), pl.BlockSpec(memory_space=pl.ANY)
    rows = n_samples * cols
    out = pl.pallas_call(
        functools.partial(kernel, n_sp, n_grp, n_core, n_parts, part_rows),
        out_shape=(
            jax.ShapeDtypeStruct(cotangent.shape, bf16),
            jax.ShapeDtypeStruct(acts.shape, bf16),
            jax.ShapeDtypeStruct((padded * channels // LANES, LANES), f32),
        ),
        in_specs=[anywhere, anywhere, in_vmem, anywhere, in_vmem, in_vmem],
        out_specs=(in_vmem, in_vmem, in_vmem),
        scratch_shapes=[
            vmem((n_rows, n_samples, cols, channels), bf16),
            vmem((n_samples, n_rows, cols, channels), bf16),
            vmem((channels, channels), bf16),
            vmem((n_rows * rows, channels), bf16),
            vmem((n_rows, rows, channels), f32),
            vmem((n_rows + 2, rows, channels), bf16),
            vmem((n_core * n_parts * part_rows, n_rows * rows), bf16),
            vmem((3, rows, channels), f32),
            vmem((n_parts, part_rows, channels), bf16),
            vmem((n_parts, part_rows, channels), bf16),
            vmem((n_parts, part_rows, channels), f32),
            vmem((n_parts, part_rows, channels), bf16),
            vmem((n_parts, part_rows, channels), bf16),
            vmem((n_core, n_parts, part_rows, channels), bf16),
            vmem((len(lane_blocks(channels)), padded, LANES), f32),
            dma((3,)),
            pltpu.SemaphoreType.REGULAR((n_parts - 2, 2)),
            dma((6,)), dma((n_sp, 2)), dma((6,)), dma((n_sp, 2)),
            dma((n_parts,)), dma((n_parts,)), dma((n_parts,)), dma((n_parts,)),
            dma((n_parts,)), dma((n_parts,)), dma((n_parts,)), dma((n_parts,)),
        ],
        compiler_params=pltpu.CompilerParams(collective_id=0, has_side_effects=True),
        name="middle_flow",
    )(acts, cotangent, depth_kernel, point_weight, gain, bias)
    return pl.pallas_call(
        finish,
        out_shape=(
            jax.ShapeDtypeStruct(cotangent.shape, bf16),
            jax.ShapeDtypeStruct(acts.shape, bf16),
            jax.ShapeDtypeStruct((width * channels,), f32),
        ),
        in_specs=[in_vmem, in_vmem, in_vmem],
        out_specs=(in_vmem, in_vmem, in_vmem),
        name="finish",
    )(*out)


def depth_forward(field, filter_weight):
    rows = field.shape[1]
    cols = field.shape[2]
    padded = jnp.pad(field, ((0, 0), (1, 1), (1, 1), (0, 0)))
    total = jnp.zeros(field.shape, jnp.float32)
    for i in range(3):
        for j in range(3):
            total = total + padded[:, i : i + rows, j : j + cols, :] * filter_weight[i, j]
    return total


def depth_backward(field, filter_weight):
    rows = field.shape[1]
    cols = field.shape[2]
    padded = jnp.pad(field, ((0, 0), (1, 1), (1, 1), (0, 0)))
    total = jnp.zeros(field.shape, jnp.float32)
    for i in range(3):
        for j in range(3):
            total = (
                total
                + padded[:, 2 - i : 2 - i + rows, 2 - j : 2 - j + cols, :] * filter_weight[i, j]
            )
    return total


def body(acts, cotangent, depth_kernel, point_weight, batch_norm_gain, norm_shift_bias):
    channel_count = acts.shape[-1]
    sample_image = lax.all_to_all(acts, "sp", split_axis=0, concat_axis=1, tiled=True)
    input_single_precision = sample_image.astype(jnp.float32)
    hidden = jnp.maximum(input_single_precision, 0.0)
    depthed = depth_forward(hidden, depth_kernel).astype(jnp.bfloat16)
    flat_d = depthed.reshape(-1, channel_count)
    element_count = flat_d.shape[0] * lax.axis_size("sp")
    projected_output = jnp.dot(flat_d, point_weight, preferred_element_type=jnp.float32)
    total, squares = lax.psum(
        (jnp.sum(projected_output, axis=0), jnp.sum(projected_output * projected_output, axis=0)),
        "sp",
    )
    batch_mean = total / element_count
    var = squares / element_count - batch_mean * batch_mean
    inverse_deviation = lax.rsqrt(var + 1e-05)
    normalized_input = (projected_output - batch_mean) * inverse_deviation
    block_out = (
        (
            input_single_precision.reshape(-1, channel_count)
            + batch_norm_gain * normalized_input
            + norm_shift_bias
        )
        .astype(jnp.bfloat16)
        .reshape(sample_image.shape)
    )
    gfloat = cotangent.astype(jnp.float32).reshape(-1, channel_count)
    scaled_output = gfloat * batch_norm_gain
    leading_layer, second_layer = lax.psum(
        (jnp.sum(scaled_output, axis=0), jnp.sum(scaled_output * normalized_input, axis=0)), "sp"
    )
    projected_gradient = (
        inverse_deviation
        * (
            scaled_output
            - leading_layer / element_count
            - normalized_input * (second_layer / element_count)
        )
    ).astype(jnp.bfloat16)
    local_weight = jnp.dot(
        flat_d.T, projected_gradient, preferred_element_type=jnp.float32
    ).reshape(-1)
    ddepth = jnp.dot(
        projected_gradient, point_weight.T, preferred_element_type=jnp.float32
    ).reshape(sample_image.shape)
    dhidden = depth_backward(ddepth, depth_kernel)
    dinput = (
        gfloat.reshape(sample_image.shape) + jnp.where(sample_image > 0, dhidden, 0.0)
    ).astype(jnp.bfloat16)
    input_grad = lax.all_to_all(dinput, "sp", split_axis=1, concat_axis=0, tiled=True)
    slices = lax.psum_scatter(
        local_weight.astype(jnp.bfloat16), "sp", scatter_dimension=0, tiled=True
    ).astype(jnp.float32)
    weight_grad = lax.psum(slices, "grp")
    return (block_out, input_grad, weight_grad)


def one_kernel_fits(mesh, acts, cotangent):
    n_sp, n_grp = mesh.shape["sp"], mesh.shape["grp"]
    group_elements = acts.size // n_grp
    return (
        acts.shape[1] == n_sp
        and acts.shape[0] == n_sp * n_grp
        and acts.shape[2] % 16 == 0
        and acts.shape[3] % n_sp == 0
        and n_grp % 4 == 0
        and n_sp == 4
        and group_elements <= 1 << 20
    )


def solution(mesh):
    in_specs = (P("grp", "sp", None, None), P(("grp", "sp"), None, None, None), P(), P(), P(), P())
    out_specs = (P(("grp", "sp"), None, None, None), P("grp", "sp", None, None), P("sp"))

    def step(acts, cotangent, *params):
        inner = fused if one_kernel_fits(mesh, acts, cotangent) else body
        mapped = jax.shard_map(
            inner, mesh=mesh, in_specs=in_specs, out_specs=out_specs, check_vma=False
        )
        return mapped(acts, cotangent, *params)

    return step
```
